128 devices in a mesh: det: 16 (over z, x), tm: 8 (over y, core).
Axes of the slice: x: 4, y: 4, z: 4, core: 2. Of those that a mesh axis runs over, the one named last changes fastest.
Arguments:
- tod: float32 [512, 8192], P('det', 'tm'), may hold values from -6 to 6
- noise_filter: float32 [8192], replicated, may hold values from 0.05 to 1
- mode_weight: float32 [32, 512], P(None, 'det'), may hold values from -0.25 to 0.25
- mode_coupling: float32 [512, 32], P('det'), may hold values from -1 to 1
- sample_weight: float32 [512, 8192], P('det', 'tm'), may hold values from 0.02 to 0.2
- pix_row: int32 [512, 8192], P('det', 'tm'), may hold values from 0 to 127, as said below
- pix_col: int32 [512, 8192], P('det', 'tm'), may hold values from 0 to 127
- angle_bin: int32 [512, 8192], P('det', 'tm'), may hold values from 0 to 63
- tile_slot: int32 [128], P('tm'), may hold values from 0 to 1
- slot_submap: int32 [8, 2], replicated, may hold values from 0 to 7, as said below
Outputs:
- signal_map: float32 [8, 3, 128, 128], P('tm', None, 'det')
- cov_map: float32 [8, 3, 3, 128, 128], P('tm', None, None, 'det')
The draws below stay inside these ranges and needn't reach their ends.
Inputs may be any that keep to these rules, and one draw needn't show every extreme that they name: `slot_submap`: the 2 entries of one row are distinct, and every submap appears in exactly 2 rows. `pix_row`: among the 1024 samples of one detector in one time group (aligned runs of 1024 samples), each band of 8 pixel rows starting at a multiple of 8 holds exactly 64 samples.
All inputs are finite; a program needn't handle non-finite values.
Results may differ from the reference program's by a relative error of at most 0.000075.
Values sent between devices are 32-bit elements; how exact they have to be, the bound alone decides.
A program may use at most 64 MiB of HBM per device.

```python
import math
import jax
import jax.numpy as jnp
from jax import lax

FILT_LEN = 8192
MODES = 32
SUBPIX = 128
ANG_BINS = 64
TILES_DEV = 16
SLOTS = 2
DETS = 512
SAMP_DEV = 1024
TILES = 128
NSUB = 8
BAND = 8
N_TM = 8


def draw_slot_submap(key, part):
    first_key, second_key = jax.random.split(jax.random.fold_in(key, 11))
    order = jax.random.permutation(first_key, NSUB)
    shifts = 1 + jax.random.permutation(second_key, NSUB - 1)
    offsets = jnp.concatenate([jnp.zeros((1,), jnp.int32), shifts[:SLOTS - 1].astype(jnp.int32)])
    groups = jnp.arange(NSUB, dtype=jnp.int32)
    return order[(groups[:, None] + offsets[None, :]) % NSUB].astype(jnp.int32)


def draw_pix_row(key, part):
    band_count = SUBPIX // BAND
    groups = FILT_LEN // SAMP_DEV
    perm_key, row_key = jax.random.split(jax.random.fold_in(key, 23))
    keys = jax.random.split(perm_key, DETS * groups)
    orders = jax.vmap(lambda single: jax.random.permutation(single, SAMP_DEV))(keys)
    band_ids = (orders % band_count).astype(jnp.int32).reshape(DETS, FILT_LEN)
    within = jax.random.randint(row_key, (DETS, FILT_LEN), 0, BAND, dtype=jnp.int32)
    return (band_ids * BAND + within).astype(jnp.int32)


def place_ends(result, own_key, least, high):
    longest = result.shape.index(max(result.shape))
    spots = []
    for shift in (0, 1):
        where = [jax.random.randint(jax.random.fold_in(own_key, axis), (), 0, length) for axis, length in enumerate(result.shape)]
        where[longest] = (where[longest] + shift) % result.shape[longest]
        spots.append(tuple(where))
    return result.at[spots[0]].set(least).at[spots[1]].set(high)


def level_of(stream_key, dims, cuts, smallest, top_value):
    factor_of, own = 1.0, jax.random.fold_in(stream_key, 6)
    for dim, shards_of in cuts:
        heights = jnp.exp(jax.random.uniform(jax.random.fold_in(own, dim), (shards_of,), jnp.float32, smallest / len(cuts), top_value / len(cuts)))
        factor_of = factor_of * jnp.repeat(heights, dims[dim] // shards_of).reshape([-1 if axis == dim else 1 for axis in range(len(dims))])
    return factor_of


def bell_draw(key, shape, width, reach, shards=(), held_as=jnp.bfloat16):
    drawn = jax.random.normal(key, shape, jnp.float32) * width
    if len(shards) > 0:
        drawn = level_of(key, shape, shards, -0.22, 0.18) * drawn
    return jnp.clip(drawn, min=-reach, max=reach).astype(held_as)


def setup_inputs(seed: int = 0) -> dict:
    arg_keys = jax.random.split(jax.random.key(seed), 11)
    tod = bell_draw(arg_keys[0], (DETS, FILT_LEN), 1.0, 6.0, ((0, 16), (1, 8)), jnp.float32)
    noise_filter = jnp.clip(jnp.exp(jax.random.uniform(arg_keys[1], (FILT_LEN,), jnp.float32, math.log(0.05), math.log(1.0))), 0.05, 1.0)
    mode_weight = bell_draw(arg_keys[2], (MODES, DETS), DETS ** -0.5, 0.25, ((1, 16),), jnp.float32)
    mode_coupling = bell_draw(arg_keys[3], (DETS, MODES), MODES ** -0.5, 1.0, ((0, 16),), jnp.float32)
    sample_weight = jnp.clip(jnp.exp(math.log(0.2) - 2.3025851 * jax.random.uniform(arg_keys[4], (DETS, FILT_LEN), jnp.float32) ** level_of(arg_keys[4], (DETS, FILT_LEN), ((0, 16), (1, 8)), -0.2, 0.2)), 0.02, 0.2)
    pix_row = draw_pix_row(jax.random.fold_in(arg_keys[10], 71), 0)
    pix_col = place_ends(jax.random.randint(arg_keys[6], (DETS, FILT_LEN), 0, SUBPIX), jax.random.fold_in(arg_keys[6], 1), 0, SUBPIX - 1).astype(jnp.int32)
    angle_bin = place_ends(jax.random.randint(arg_keys[7], (DETS, FILT_LEN), 0, ANG_BINS), jax.random.fold_in(arg_keys[7], 1), 0, ANG_BINS - 1).astype(jnp.int32)
    tile_slot = place_ends(jax.random.randint(arg_keys[8], (TILES,), 0, SLOTS), jax.random.fold_in(arg_keys[8], 1), 0, SLOTS - 1).astype(jnp.int32)
    slot_submap = draw_slot_submap(jax.random.fold_in(arg_keys[10], 71), 0)
    return dict(tod=tod, noise_filter=noise_filter, mode_weight=mode_weight, mode_coupling=mode_coupling, sample_weight=sample_weight, pix_row=pix_row, pix_col=pix_col, angle_bin=angle_bin, tile_slot=tile_slot, slot_submap=slot_submap)


highest = lax.Precision.HIGHEST


def reference(tod, noise_filter, mode_weight, mode_coupling, sample_weight, pix_row, pix_col, angle_bin, tile_slot, slot_submap):
    spectrum = jnp.fft.fft(tod, axis=1)
    filtered = jnp.real(jnp.fft.ifft(spectrum * noise_filter[None, :], axis=1)).astype(jnp.float32)
    mode_amps = jnp.dot(mode_weight, filtered, precision=highest, preferred_element_type=jnp.float32)
    cleaned = filtered - jnp.dot(mode_coupling, mode_amps, precision=highest, preferred_element_type=jnp.float32)
    angles = angle_bin.astype(jnp.float32) * (2.0 * math.pi / ANG_BINS)
    cosine = jnp.cos(angles)
    sine_part = jnp.sin(angles)
    sample_time = jnp.arange(FILT_LEN, dtype=jnp.int32)
    samp_dev = FILT_LEN // N_TM
    tile_size = samp_dev // TILES_DEV
    slot_of = tile_slot[sample_time // tile_size]
    submap = slot_submap[sample_time // samp_dev, slot_of]
    pixel_index = ((submap[None, :] * SUBPIX + pix_row) * SUBPIX + pix_col).reshape(-1).astype(jnp.int32)
    cell_count = NSUB * SUBPIX * SUBPIX

    def pixel_sum(values):
        summed = jax.ops.segment_sum(values.reshape(-1), pixel_index, num_segments=cell_count)
        return summed.reshape(NSUB, SUBPIX, SUBPIX)

    factors = [jnp.ones_like(cosine), cosine, sine_part]
    weighted = sample_weight * cleaned
    signal = jnp.stack([pixel_sum(weighted * col_factor) for col_factor in factors], axis=1)
    covariance = jnp.stack([jnp.stack([pixel_sum(sample_weight * row_factor * col_factor) for col_factor in factors], axis=1) for row_factor in factors], axis=1)
    return signal, covariance
```

```python
import math

import jax
import jax.numpy as jnp
import numpy as np
from jax import lax
from jax.experimental import pallas as pl
from jax.experimental.pallas import tpu as pltpu
from jax.sharding import PartitionSpec as P

F32 = jnp.float32
BF16 = jnp.bfloat16
MESH = pl.DeviceIdType.MESH
ND = 16
NT = 8


def split_const(table):
    hi = table.astype(jnp.bfloat16)
    lo = (table - hi.astype(np.float64)).astype(jnp.bfloat16)
    return hi, lo


def dft_tables():
    one = np.arange(64)
    ang = 2.0 * math.pi * (np.outer(one, one) % 64) / 64
    first = np.concatenate([np.cos(ang), -np.sin(ang)], 0)
    lane = np.arange(128)
    k2 = 2 * (lane % 64) + lane // 64
    ang = 2.0 * math.pi * (np.outer(lane, k2) % 128) / 128
    co, si = np.cos(ang), np.sin(ang)
    second = np.block([[co, -si], [si, co]])
    third = np.block([[co.T, si.T], [-si.T, co.T]])
    ang = 2.0 * math.pi * np.outer(one, lane) / 8192
    turn = np.stack([np.cos(ang), np.sin(ang)]).astype(np.float32)
    return first, first.T / 8192.0, second, third, turn


def split(value):
    hi = value.astype(BF16)
    lo = (value - hi.astype(F32)).astype(BF16)
    return hi, lo


def mm(a, b):
    return lax.dot_general(a, b, (((1,), (0,)), ((), ())), preferred_element_type=F32)


def dot3(a, b):
    return mm(a[0], b[0]) + (mm(a[0], b[1]) + mm(a[1], b[0]))


def signal_all(me_d, me_t):
    barrier = pltpu.get_barrier_semaphore()
    for i in range(1, ND):
        pl.semaphore_signal(
            barrier, inc=1, device_id={"det": (me_d + i) % ND}, device_id_type=MESH
        )
    for i in range(1, NT):
        pl.semaphore_signal(
            barrier, inc=1, device_id={"tm": (me_t + i) % NT}, device_id_type=MESH
        )
    pl.semaphore_wait(barrier, ND - 1 + NT - 1)


def exchange(axis, size, me, src_of, dst_buf, send_sem, recv_sem):
    copies = []
    for i in range(1, size):
        peer = (me + i) % size
        copy = pltpu.make_async_remote_copy(
            src_ref=src_of(peer),
            dst_ref=dst_buf.at[me],
            send_sem=send_sem.at[peer],
            recv_sem=recv_sem.at[me],
            device_id={axis: peer},
            device_id_type=MESH,
        )
        copy.start()
        copies.append(copy)
    return copies


def arrive(axis, size, me, dst_buf, send_sem, recv_sem):
    for i in range(1, size):
        peer = (me + i) % size
        pltpu.make_async_remote_copy(
            src_ref=dst_buf.at[peer],
            dst_ref=dst_buf.at[peer],
            send_sem=send_sem.at[peer],
            recv_sem=recv_sem.at[peer],
            device_id={axis: peer},
            device_id_type=MESH,
        ).wait_recv()


def filter_kernel(
    tod,
    gain,
    weight,
    couple,
    ah,
    al,
    ih,
    il,
    bh,
    bl,
    ch,
    cl,
    turn,
    out,
    ybuf,
    rbuf,
    zbuf,
    zall,
    sbuf,
    xin,
    obuf,
    cin,
    s1,
    r1,
    s2,
    r2,
    s3,
    r3,
    s4,
    r4,
):
    me_d = lax.axis_index("det")
    me_t = lax.axis_index("tm")
    signal_all(me_d, me_t)
    wsp = split(weight[...])
    for a in range(8):
        y = dot3(wsp, split(tod[:, 128 * a : 128 * a + 128]))
        ybuf[2 * a] = y[:16]
        ybuf[2 * a + 1] = y[16:]
    copies = exchange("det", ND, me_d, lambda p: ybuf.at[p], rbuf, s1, r1)
    g = gain[...]
    gfull = jnp.concatenate([g[:, :64].T, g[:, 64:].T], axis=1)
    rbuf[me_d] = ybuf[me_d]
    arrive("det", ND, me_d, rbuf, s1, r1)
    total = rbuf[0]
    for i in range(1, ND):
        total = total + rbuf[i]
    zbuf[...] = total
    for c in copies:
        c.wait_send()
    copies = exchange("det", ND, me_d, lambda p: zbuf, zall, s2, r2)
    zall[me_d] = total
    csp = split(couple[...])
    arrive("det", ND, me_d, zall, s2, r2)
    cleaned = []
    for a in range(8):
        modes = jnp.concatenate([zall[2 * a], zall[2 * a + 1]], axis=0)
        cleaned.append(tod[:, 128 * a : 128 * a + 128] - dot3(csp, split(modes)))
    turned = jnp.stack(cleaned, axis=1)
    sbuf[...] = turned.reshape(NT, 4, 8, 128)
    for c in copies:
        c.wait_send()
    copies = exchange("tm", NT, me_t, lambda p: sbuf.at[p], xin, s3, r3)
    xin[me_t] = sbuf[me_t]
    arrive("tm", NT, me_t, xin, s3, r3)
    cols = [
        jnp.concatenate([xin[m, e] for m in range(NT)], axis=0) for e in range(4)
    ]
    x = jnp.concatenate(cols, axis=1)
    f = dot3((ah[...], al[...]), split(x))
    tc, ts = turn[0], turn[1]
    rows = []
    for e in range(4):
        re, im = f[:64, 128 * e : 128 * e + 128], f[64:, 128 * e : 128 * e + 128]
        rows.append(jnp.concatenate([re * tc + im * ts, im * tc - re * ts], axis=1))
    f = dot3(split(jnp.concatenate(rows, axis=0)), (bh[...], bl[...]))
    gg = jnp.concatenate([gfull, gfull], axis=1)
    f = f * jnp.concatenate([gg] * 4, axis=0)
    f = dot3(split(f), (ch[...], cl[...]))
    cols = []
    for e in range(4):
        re, im = f[64 * e : 64 * e + 64, :128], f[64 * e : 64 * e + 64, 128:]
        cols.append(jnp.concatenate([re * tc - im * ts, im * tc + re * ts], axis=0))
    f = dot3((ih[...], il[...]), split(jnp.concatenate(cols, axis=1)))
    for m in range(NT):
        for e in range(4):
            obuf[m, e] = f[8 * m : 8 * m + 8, 128 * e : 128 * e + 128]
    for c in copies:
        c.wait_send()
    copies = exchange("tm", NT, me_t, lambda p: obuf.at[p], cin, s4, r4)
    cin[me_t] = obuf[me_t]
    arrive("tm", NT, me_t, cin, s4, r4)
    back = cin[...].reshape(32, 8, 128)
    for a in range(8):
        out[:, 128 * a : 128 * a + 128] = back[:, a]
    for c in copies:
        c.wait_send()


def trig(ang):
    h = (ang - 32).astype(F32) * np.float32(np.pi / 64)
    x = h * h
    s = np.float32(-1 / 39916800)
    for k in (1 / 362880, -1 / 5040, 1 / 120, -1 / 6, 1.0):
        s = s * x + np.float32(k)
    s = s * h
    c = np.float32(1 / 479001600)
    for k in (-1 / 3628800, 1 / 40320, -1 / 720, 1 / 24, -1 / 2, 1.0):
        c = c * x + np.float32(k)
    return 2.0 * s * s - 1.0, -2.0 * s * c


def pairs(x):
    lane = lax.broadcasted_iota(jnp.int32, (16, 128), 1)
    u, v = x[:16], x[16:]
    ur = pltpu.roll(u, 64, 1)
    vr = pltpu.roll(v, 64, 1)
    return jnp.where(lane < 64, u, vr), jnp.where(lane < 64, ur, v)


def hist_kernel(slots, w_ref, cl_ref, row_ref, col_ref, ang_ref, out, val, mi, ni, term, lt, rt):
    for a in range(8):
        sl = slice(128 * a, 128 * a + 128)
        w = w_ref[:, sl]
        c, s = trig(ang_ref[:, sl])
        g = w * cl_ref[:, sl]
        wc = w * c
        for q, v in enumerate((w, wc, w * s, wc * c, wc * s, g, g * c, g * s)):
            hi = v.astype(BF16).astype(F32)
            for k, part in enumerate((hi, v - hi)):
                val[2 * q + k, 2 * a], val[2 * q + k, 2 * a + 1] = pairs(part)
        row = row_ref[:, sl]
        mi[2 * a], mi[2 * a + 1] = pairs((row % 64).astype(F32))
        ni[2 * a], ni[2 * a + 1] = pairs((row // 64 * 128 + col_ref[:, sl]).astype(F32))
    im = lax.broadcasted_iota(jnp.int32, (64, 128), 0).astype(F32).astype(BF16)
    it = lax.broadcasted_iota(jnp.int32, (256, 128), 0).astype(F32).astype(BF16)

    def tile(j, carry):
        for k in range(16):
            lanes = slice(128 * k, 128 * k + 128)
            mask = jnp.broadcast_to(mi[j, k : k + 1, :], (64, 128)).astype(BF16) == im
            for q in range(16):
                vb = jnp.broadcast_to(val[q, j, k : k + 1, :], (64, 128)).astype(BF16)
                lt[64 * q : 64 * q + 64, lanes] = jnp.where(mask, vb, jnp.zeros_like(vb))
            nb = jnp.broadcast_to(ni[j, k : k + 1, :], (256, 128)).astype(BF16)
            rt[:, lanes] = jnp.where(nb == it, jnp.ones_like(nb), jnp.zeros_like(nb))
        acc = lax.dot_general(
            lt[...], rt[...], (((1,), (1,)), ((), ())), preferred_element_type=F32
        ).reshape(8, 2, 64, 256)
        term[j] = acc[:, 0] + acc[:, 1]
        return carry

    lax.fori_loop(0, 16, tile, 0)
    for q in range(8):
        for h in range(2):

            def total(j, carry):
                second = slots[j].astype(F32)
                t = term[j, q, :, 128 * h : 128 * h + 128]
                return carry[0] + t * (1.0 - second), carry[1] + t * second

            zero = jnp.zeros((64, 128), F32)
            first, second = lax.fori_loop(0, 16, total, (zero, zero))
            out[0, q, 64 * h : 64 * h + 64, :] = first
            out[1, q, 64 * h : 64 * h + 64, :] = second


def reduce_kernel(sub, maps, signal, cov, rbuf, tbuf, ubuf, s1, r1, s2, r2):
    me_d = lax.axis_index("det")
    me_t = lax.axis_index("tm")
    signal_all(me_d, me_t)

    def band(p):
        return maps.at[:, :, pl.ds(pl.multiple_of(8 * p, 8), 8), :]

    copies = exchange("det", ND, me_d, band, rbuf, s1, r1)
    rbuf[me_d] = maps[:, :, pl.ds(pl.multiple_of(8 * me_d, 8), 8), :]
    arrive("det", ND, me_d, rbuf, s1, r1)
    sub0 = sub[me_t, 0]
    sub1 = sub[me_t, 1]
    for q in range(8):
        a0 = rbuf[0, 0, q]
        a1 = rbuf[0, 1, q]
        for i in range(1, ND):
            a0 = a0 + rbuf[i, 0, q]
            a1 = a1 + rbuf[i, 1, q]
        for n in range(NT):
            tbuf[n, q] = jnp.where(sub0 == n, a0, 0.0) + jnp.where(sub1 == n, a1, 0.0)
    for c in copies:
        c.wait_send()
    copies = exchange("tm", NT, me_t, lambda p: tbuf.at[p], ubuf, s2, r2)
    ubuf[me_t] = tbuf[me_t]
    arrive("tm", NT, me_t, ubuf, s2, r2)
    tot = []
    for q in range(8):
        a = ubuf[0, q]
        for i in range(1, NT):
            a = a + ubuf[i, q]
        tot.append(a)
    for q in range(3):
        signal[0, q] = tot[5 + q]
    w, wc, ws, wcc, wcs = tot[:5]
    full = ((w, wc, ws), (wc, wcc, wcs), (ws, wcs, w - wcc))
    for i in range(3):
        for j in range(3):
            cov[0, i, j] = full[i][j]
    for c in copies:
        c.wait_send()


def body(
    tod,
    noise_filter,
    mode_weight,
    mode_coupling,
    sample_weight,
    pix_row,
    pix_col,
    angle_bin,
    tile_slot,
    slot_submap,
):
    vm = pl.BlockSpec(memory_space=pltpu.VMEM)
    sm = pl.BlockSpec(memory_space=pltpu.SMEM)
    dma = pltpu.SemaphoreType.DMA
    first, last, second, third, turn = dft_tables()
    tables = [jnp.asarray(t) for m in (first, last, second, third) for t in split_const(m)]
    cleaned = pl.pallas_call(
        filter_kernel,
        out_shape=jax.ShapeDtypeStruct((32, 1024), F32),
        in_specs=[vm] * 13,
        out_specs=vm,
        scratch_shapes=[
            pltpu.VMEM((ND, 16, 128), F32),
            pltpu.VMEM((ND, 16, 128), F32),
            pltpu.VMEM((16, 128), F32),
            pltpu.VMEM((ND, 16, 128), F32),
            pltpu.VMEM((NT, 4, 8, 128), F32),
            pltpu.VMEM((NT, 4, 8, 128), F32),
            pltpu.VMEM((NT, 4, 8, 128), F32),
            pltpu.VMEM((NT, 4, 8, 128), F32),
            dma((ND,)),
            dma((ND,)),
            dma((ND,)),
            dma((ND,)),
            dma((NT,)),
            dma((NT,)),
            dma((NT,)),
            dma((NT,)),
        ],
        compiler_params=pltpu.CompilerParams(collective_id=0, has_side_effects=True),
    )(
        tod,
        noise_filter.reshape(64, 128),
        mode_weight,
        mode_coupling,
        *tables,
        jnp.asarray(turn),
    )
    maps = pl.pallas_call(
        hist_kernel,
        out_shape=jax.ShapeDtypeStruct((2, 8, 128, 128), F32),
        in_specs=[sm] + [vm] * 5,
        out_specs=vm,
        scratch_shapes=[
            pltpu.VMEM((16, 16, 16, 128), F32),
            pltpu.VMEM((16, 16, 128), F32),
            pltpu.VMEM((16, 16, 128), F32),
            pltpu.VMEM((16, 8, 64, 256), F32),
            pltpu.VMEM((1024, 2048), BF16),
            pltpu.VMEM((256, 2048), BF16),
        ],
        compiler_params=pltpu.CompilerParams(vmem_limit_bytes=56 << 20),
    )(tile_slot, sample_weight, cleaned, pix_row, pix_col, angle_bin)
    return pl.pallas_call(
        reduce_kernel,
        out_shape=(
            jax.ShapeDtypeStruct((1, 3, 8, 128), F32),
            jax.ShapeDtypeStruct((1, 3, 3, 8, 128), F32),
        ),
        in_specs=[sm, vm],
        out_specs=(vm, vm),
        scratch_shapes=[
            pltpu.VMEM((ND, 2, 8, 8, 128), F32),
            pltpu.VMEM((NT, 8, 8, 128), F32),
            pltpu.VMEM((NT, 8, 8, 128), F32),
            dma((ND,)),
            dma((ND,)),
            dma((NT,)),
            dma((NT,)),
        ],
        compiler_params=pltpu.CompilerParams(collective_id=1, has_side_effects=True),
    )(slot_submap, maps)


def solution(mesh):
    return jax.shard_map(
        body,
        mesh=mesh,
        in_specs=(
            P("det", "tm"),
            P(),
            P(None, "det"),
            P("det", None),
            P("det", "tm"),
            P("det", "tm"),
            P("det", "tm"),
            P("det", "tm"),
            P("tm"),
            P(),
        ),
        out_specs=(P("tm", None, "det", None), P("tm", None, None, "det", None)),
        check_vma=False,
    )
```

```python
import math

import jax
import jax.numpy as jnp
import numpy as np
from jax import lax
from jax.experimental import pallas as pl
from jax.experimental.pallas import tpu as pltpu
from jax.sharding import PartitionSpec as P

F32 = jnp.float32
BF16 = jnp.bfloat16
MESH = pl.DeviceIdType.MESH
ND = 16
NT = 8
CUTS = (0, 6, 10, 16)


def split_const(table):
    hi = table.astype(jnp.bfloat16)
    lo = (table - hi.astype(np.float64)).astype(jnp.bfloat16)
    return hi, lo


def dft_tables():
    one = np.arange(64)
    ang = 2.0 * math.pi * (np.outer(one, one) % 64) / 64
    first = np.concatenate([np.cos(ang), -np.sin(ang)], 0)
    lane = np.arange(128)
    k2 = 2 * (lane % 64) + lane // 64
    ang = 2.0 * math.pi * (np.outer(lane, k2) % 128) / 128
    co, si = np.cos(ang), np.sin(ang)
    second = np.block([[co, -si], [si, co]])
    third = np.block([[co.T, si.T], [-si.T, co.T]])
    ang = 2.0 * math.pi * np.outer(one, lane) / 8192
    turn = np.stack([np.cos(ang), np.sin(ang)]).astype(np.float32)
    return first, first.T / 8192.0, second, third, turn


def split(value):
    hi = value.astype(BF16)
    lo = (value - hi.astype(F32)).astype(BF16)
    return hi, lo


def mm(a, b):
    return lax.dot_general(a, b, (((1,), (0,)), ((), ())), preferred_element_type=F32)


def dot3(a, b):
    return mm(a[0], b[0]) + (mm(a[0], b[1]) + mm(a[1], b[0]))


def greet(me_d, me_t):
    barrier = pltpu.get_barrier_semaphore()
    for i in range(1, ND):
        pl.semaphore_signal(
            barrier, inc=1, device_id={"det": (me_d + i) % ND}, device_id_type=MESH
        )
    for i in range(1, NT):
        pl.semaphore_signal(
            barrier, inc=1, device_id={"tm": (me_t + i) % NT}, device_id_type=MESH
        )
    return barrier


def send(axis, size, me, src_of, dst_buf, sems):
    copies = []
    for i in range(1, size):
        peer = (me + i) % size
        copy = pltpu.make_async_remote_copy(
            src_ref=src_of(peer),
            dst_ref=dst_buf.at[me],
            send_sem=sems.at[0, peer],
            recv_sem=sems.at[1, me],
            device_id={axis: peer},
            device_id_type=MESH,
        )
        copy.start()
        copies.append(copy)
    return copies


def arrive(axis, size, me, dst_buf, sems):
    for i in range(1, size):
        peer = (me + i) % size
        pltpu.make_async_remote_copy(
            src_ref=dst_buf.at[peer],
            dst_ref=dst_buf.at[peer],
            send_sem=sems.at[0, peer],
            recv_sem=sems.at[1, peer],
            device_id={axis: peer},
            device_id_type=MESH,
        ).wait_recv()


def trig(ang):
    h = (ang - 32).astype(F32) * np.float32(np.pi / 64)
    x = h * h
    s = np.float32(-1 / 39916800)
    for k in (1 / 362880, -1 / 5040, 1 / 120, -1 / 6, 1.0):
        s = s * x + np.float32(k)
    s = s * h
    c = np.float32(1 / 479001600)
    for k in (-1 / 3628800, 1 / 40320, -1 / 720, 1 / 24, -1 / 2, 1.0):
        c = c * x + np.float32(k)
    return 2.0 * s * s - 1.0, -2.0 * s * c


def pairs(x):
    lane = lax.broadcasted_iota(jnp.int32, (16, 128), 1)
    u, v = x[:16], x[16:]
    ur = pltpu.roll(u, 64, 1)
    vr = pltpu.roll(v, 64, 1)
    return jnp.where(lane < 64, u, vr), jnp.where(lane < 64, ur, v)


def put(val, a, values):
    for q, v in enumerate(values):
        hi = v.astype(BF16).astype(F32)
        for k, part in enumerate((hi, v - hi)):
            val[2 * q + k, 2 * a], val[2 * q + k, 2 * a + 1] = pairs(part)


def tile_sum(j, count, val, mi, lt, rt, term):
    im = lax.broadcasted_iota(jnp.int32, (64, 128), 0).astype(F32).astype(BF16)
    for k in range(16):
        mask = jnp.broadcast_to(mi[j, k : k + 1, :], (64, 128)).astype(BF16) == im
        for q in range(2 * count):
            vb = jnp.broadcast_to(val[q, j, k : k + 1, :], (64, 128)).astype(BF16)
            lt[k, 64 * q : 64 * q + 64, :] = jnp.where(mask, vb, jnp.zeros_like(vb))
    left = jnp.concatenate([lt[k] for k in range(16)], axis=1)
    right = jnp.concatenate([rt[j, k] for k in range(16)], axis=1)
    acc = lax.dot_general(
        left, right, (((1,), (1,)), ((), ())), preferred_element_type=F32
    ).reshape(count, 2, 64, 256)
    term[j] = acc[:, 0] + acc[:, 1]


def columns(j, ni, rt):
    it = lax.broadcasted_iota(jnp.int32, (256, 128), 0).astype(F32).astype(BF16)
    for k in range(16):
        nb = jnp.broadcast_to(ni[j, k : k + 1, :], (256, 128)).astype(BF16)
        rt[j, k] = jnp.where(nb == it, jnp.ones_like(nb), jnp.zeros_like(nb))


def by_slot(slots, term, count, maps):
    marks = [slots[j].astype(F32) for j in range(16)]
    for h in range(2):

        def one(q, carry):
            every = jnp.zeros((64, 128), F32)
            second = jnp.zeros((64, 128), F32)
            for j in range(16):
                t = term[j, q, :, 128 * h : 128 * h + 128]
                every = every + t
                second = second + t * marks[j]
            first = every - second
            for b in range(8):
                maps[8 * h + b, 0, q] = first[8 * b : 8 * b + 8]
                maps[8 * h + b, 1, q] = second[8 * b : 8 * b + 8]
            return carry

        lax.fori_loop(0, count, one, 0)


def spread(sub0, sub1, count, got, out):
    for q in range(count):
        a0 = got[0, 0, q]
        a1 = got[0, 1, q]
        for i in range(1, ND):
            a0 = a0 + got[i, 0, q]
            a1 = a1 + got[i, 1, q]
        for n in range(NT):
            out[n, q] = jnp.where(sub0 == n, a0, 0.0) + jnp.where(sub1 == n, a1, 0.0)


def noise_filtering(x, g, ah, al, bh, bl, ch, cl, ih, il, turn):
    count = x.shape[1] // 128
    tc, ts = turn[0], turn[1]
    f = dot3((ah[...], al[...]), split(x))
    rows = []
    for e in range(count):
        re, im = f[:64, 128 * e : 128 * e + 128], f[64:, 128 * e : 128 * e + 128]
        rows.append(jnp.concatenate([re * tc + im * ts, im * tc - re * ts], axis=1))
    f = dot3(split(jnp.concatenate(rows, axis=0)), (bh[...], bl[...]))
    gg = jnp.concatenate([g, g], axis=1)
    f = f * jnp.concatenate([gg] * count, axis=0)
    f = dot3(split(f), (ch[...], cl[...]))
    cols = []
    for e in range(count):
        re, im = f[64 * e : 64 * e + 64, :128], f[64 * e : 64 * e + 64, 128:]
        cols.append(jnp.concatenate([re * tc - im * ts, im * tc + re * ts], axis=0))
    return dot3((ih[...], il[...]), split(jnp.concatenate(cols, axis=1)))


def fused_kernel(
    slots,
    sub,
    tod,
    gain,
    weight,
    couple,
    w_ref,
    row_ref,
    col_ref,
    ang_ref,
    ah,
    al,
    ih,
    il,
    bh,
    bl,
    ch,
    cl,
    turn,
    out,
    ybuf,
    yin,
    sbuf,
    xin,
    zbuf,
    zin,
    fbuf,
    fin,
    ftmp,
    obuf,
    cin,
    wcs,
    valc,
    vals,
    mi,
    ni,
    ltc,
    lts,
    rt,
    termc,
    terms,
    mapc,
    maps,
    rsc,
    rss,
    tbc,
    tbs,
    ubc,
    ubs,
    sy,
    sx,
    sz,
    sf,
    so,
    sc,
    ss,
    tc_sem,
    ts_sem,
):
    me_d = lax.axis_index("det")
    me_t = lax.axis_index("tm")
    barrier = greet(me_d, me_t)
    wsp = split(weight[...])
    for a in range(8):
        x = tod[:, 128 * a : 128 * a + 128]
        ybuf[:, a, :] = dot3(wsp, split(x))
        sbuf[:, a, :] = x
    pl.semaphore_wait(barrier, ND - 1 + NT - 1)
    copies = send("det", ND, me_d, lambda p: ybuf.at[pl.ds(2 * p, 2)], yin, sy)
    copies += send("tm", NT, me_t, lambda p: sbuf.at[pl.ds(4 * p, 4)], xin, sx)
    yin[me_d] = ybuf[pl.ds(2 * me_d, 2)]
    xin[me_t] = sbuf[pl.ds(4 * me_t, 4)]
    g = gain[...]
    gfull = jnp.concatenate([g[:, :64].T, g[:, 64:].T], axis=1)
    for a in range(8):
        sl = slice(128 * a, 128 * a + 128)
        w = w_ref[:, sl]
        c, s = trig(ang_ref[:, sl])
        wc = w * c
        ws = w * s
        wcs[0, a] = wc
        wcs[1, a] = ws
        put(valc, a, (w, wc, ws, wc * c, wc * s))
        row = row_ref[:, sl]
        mi[2 * a], mi[2 * a + 1] = pairs((row % 64).astype(F32))
        ni[2 * a], ni[2 * a + 1] = pairs((row // 64 * 128 + col_ref[:, sl]).astype(F32))

    def cov_tile(j, carry):
        columns(j, ni, rt)
        tile_sum(j, 5, valc, mi, ltc, rt, termc)
        return carry

    lax.fori_loop(CUTS[0], CUTS[1], cov_tile, 0)
    arrive("det", ND, me_d, yin, sy)
    z = yin[0]
    for i in range(1, ND):
        z = z + yin[i]
    zbuf[...] = z
    copies += send("tm", NT, me_t, lambda p: zbuf, zin, sz)
    zin[me_t] = z
    lax.fori_loop(CUTS[1], CUTS[2], cov_tile, 0)
    arrive("tm", NT, me_t, xin, sx)
    arrive("tm", NT, me_t, zin, sz)
    cols = [jnp.concatenate([xin[m, e] for m in range(NT)], axis=0) for e in range(4)]
    cols += [jnp.concatenate([zin[m, e] for m in range(NT)], axis=0) for e in range(2)]
    f = noise_filtering(
        jnp.concatenate(cols, axis=1), gfull, ah, al, bh, bl, ch, cl, ih, il, turn
    )
    for m in range(NT):
        for e in range(4):
            obuf[m, e] = f[8 * m : 8 * m + 8, 128 * e : 128 * e + 128]
        for e in range(2):
            ftmp[m, e] = f[8 * m : 8 * m + 8, 512 + 128 * e : 640 + 128 * e]
    mine = ftmp[me_t]
    fbuf[...] = mine
    copies += send("det", ND, me_d, lambda p: fbuf, fin, sf)
    copies += send("tm", NT, me_t, lambda p: obuf.at[p], cin, so)
    fin[me_d] = mine
    cin[me_t] = obuf[me_t]
    lax.fori_loop(CUTS[2], CUTS[3], cov_tile, 0)
    by_slot(slots, termc, 5, mapc)
    copies += send("det", ND, me_d, lambda p: mapc.at[p], rsc, sc)
    rsc[me_d] = mapc[me_d]
    arrive("det", ND, me_d, fin, sf)
    arrive("tm", NT, me_t, cin, so)
    csp = split(couple[...])
    for a in range(8):
        modes = fin[:, :, a, :].reshape(32, 128)
        clean = cin[:, :, a, :].reshape(32, 128) - dot3(csp, split(modes))
        w = w_ref[:, 128 * a : 128 * a + 128]
        put(vals, a, (w * clean, wcs[0, a] * clean, wcs[1, a] * clean))

    def signal_tile(j, carry):
        tile_sum(j, 3, vals, mi, lts, rt, terms)
        return carry

    lax.fori_loop(0, 16, signal_tile, 0)
    by_slot(slots, terms, 3, maps)
    copies += send("det", ND, me_d, lambda p: maps.at[p], rss, ss)
    rss[me_d] = maps[me_d]
    sub0 = sub[me_t, 0]
    sub1 = sub[me_t, 1]
    arrive("det", ND, me_d, rsc, sc)
    spread(sub0, sub1, 5, rsc, tbc)
    copies += send("tm", NT, me_t, lambda p: tbc.at[p], ubc, tc_sem)
    ubc[me_t] = tbc[me_t]
    arrive("det", ND, me_d, rss, ss)
    spread(sub0, sub1, 3, rss, tbs)
    copies += send("tm", NT, me_t, lambda p: tbs.at[p], ubs, ts_sem)
    ubs[me_t] = tbs[me_t]
    arrive("tm", NT, me_t, ubc, tc_sem)
    total = ubc[0]
    for i in range(1, NT):
        total = total + ubc[i]
    out[:5] = total
    arrive("tm", NT, me_t, ubs, ts_sem)
    total = ubs[0]
    for i in range(1, NT):
        total = total + ubs[i]
    out[5:] = total
    for c in copies:
        c.wait_send()


def finish_kernel(tot, signal, cov):
    for q in range(3):
        signal[0, q] = tot[5 + q]
    w, wc, ws, wcc, wcs = (tot[q] for q in range(5))
    full = ((w, wc, ws), (wc, wcc, wcs), (ws, wcs, w - wcc))
    for i in range(3):
        for j in range(3):
            cov[0, i, j] = full[i][j]


def body(
    tod,
    noise_filter,
    mode_weight,
    mode_coupling,
    sample_weight,
    pix_row,
    pix_col,
    angle_bin,
    tile_slot,
    slot_submap,
):
    vm = pl.BlockSpec(memory_space=pltpu.VMEM)
    sm = pl.BlockSpec(memory_space=pltpu.SMEM)
    first, last, second, third, turn = dft_tables()
    ah, al = split_const(first)
    ih, il = split_const(last)
    bh, bl = split_const(second)
    ch, cl = split_const(third)
    tables = [jnp.asarray(t) for t in (ah, al, ih, il, bh, bl, ch, cl, turn)]

    def vmem(*shape, dtype=F32):
        return pltpu.VMEM(shape, dtype)

    def sems(size):
        return pltpu.SemaphoreType.DMA((2, size))

    tot = pl.pallas_call(
        fused_kernel,
        out_shape=jax.ShapeDtypeStruct((8, 8, 128), F32),
        in_specs=[sm, sm] + [vm] * 17,
        out_specs=vm,
        scratch_shapes=[
            vmem(32, 8, 128),
            vmem(ND, 2, 8, 128),
            vmem(32, 8, 128),
            vmem(NT, 4, 8, 128),
            vmem(2, 8, 128),
            vmem(NT, 2, 8, 128),
            vmem(2, 8, 128),
            vmem(ND, 2, 8, 128),
            vmem(NT, 2, 8, 128),
            vmem(NT, 4, 8, 128),
            vmem(NT, 4, 8, 128),
            vmem(2, 8, 32, 128),
            vmem(10, 16, 16, 128),
            vmem(6, 16, 16, 128),
            vmem(16, 16, 128),
            vmem(16, 16, 128),
            vmem(16, 640, 128, dtype=BF16),
            vmem(16, 384, 128, dtype=BF16),
            vmem(16, 16, 256, 128, dtype=BF16),
            vmem(16, 5, 64, 256),
            vmem(16, 3, 64, 256),
            vmem(ND, 2, 5, 8, 128),
            vmem(ND, 2, 3, 8, 128),
            vmem(ND, 2, 5, 8, 128),
            vmem(ND, 2, 3, 8, 128),
            vmem(NT, 5, 8, 128),
            vmem(NT, 3, 8, 128),
            vmem(NT, 5, 8, 128),
            vmem(NT, 3, 8, 128),
            sems(ND),
            sems(NT),
            sems(NT),
            sems(ND),
            sems(NT),
            sems(ND),
            sems(ND),
            sems(NT),
            sems(NT),
        ],
        compiler_params=pltpu.CompilerParams(
            collective_id=0, has_side_effects=True, vmem_limit_bytes=56 << 20
        ),
    )(
        tile_slot,
        slot_submap,
        tod,
        noise_filter.reshape(64, 128),
        mode_weight,
        mode_coupling,
        sample_weight,
        pix_row,
        pix_col,
        angle_bin,
        *tables,
    )
    return pl.pallas_call(
        finish_kernel,
        out_shape=(
            jax.ShapeDtypeStruct((1, 3, 8, 128), F32),
            jax.ShapeDtypeStruct((1, 3, 3, 8, 128), F32),
        ),
        in_specs=[vm],
        out_specs=(vm, vm),
    )(tot)


def solution(mesh):
    return jax.shard_map(
        body,
        mesh=mesh,
        in_specs=(
            P("det", "tm"),
            P(),
            P(None, "det"),
            P("det", None),
            P("det", "tm"),
            P("det", "tm"),
            P("det", "tm"),
            P("det", "tm"),
            P("tm"),
            P(),
        ),
        out_specs=(P("tm", None, "det", None), P("tm", None, None, "det", None)),
        check_vma=False,
    )
```

```python
import math

import jax
import jax.numpy as jnp
import numpy as np
from jax import lax
from jax.experimental import pallas as pl
from jax.experimental.pallas import tpu as pltpu
from jax.sharding import PartitionSpec as P

F32 = jnp.float32
BF16 = jnp.bfloat16
MESH = pl.DeviceIdType.MESH
ND = 16
NT = 8
GROUP = 8
CUTS = (0, 1, 4)
STEPS = (0, 4, 8)


def split_const(table):
    hi = table.astype(jnp.bfloat16)
    lo = (table - hi.astype(np.float64)).astype(jnp.bfloat16)
    return hi, lo


def dft_tables():
    one = np.arange(64)
    ang = 2.0 * math.pi * (np.outer(one, one) % 64) / 64
    first = np.concatenate([np.cos(ang), -np.sin(ang)], 0)
    lane = np.arange(128)
    k2 = 2 * (lane % 64) + lane // 64
    ang = 2.0 * math.pi * (np.outer(lane, k2) % 128) / 128
    co, si = np.cos(ang), np.sin(ang)
    second = np.block([[co, -si], [si, co]])
    third = np.block([[co.T, si.T], [-si.T, co.T]])
    ang = 2.0 * math.pi * np.outer(one, lane) / 8192
    turn = np.stack([np.cos(ang), np.sin(ang)]).astype(np.float32)
    return first, first.T / 8192.0, second, third, turn


def split(value):
    hi = value.astype(BF16)
    lo = (value - hi.astype(F32)).astype(BF16)
    return hi, lo


def mm(a, b):
    return lax.dot_general(a, b, (((1,), (0,)), ((), ())), preferred_element_type=F32)


def dot3(a, b):
    return mm(a[0], b[0]) + (mm(a[0], b[1]) + mm(a[1], b[0]))


def greet(me_d, me_t):
    barrier = pltpu.get_barrier_semaphore()
    for i in range(1, ND):
        pl.semaphore_signal(
            barrier, inc=1, device_id={"det": (me_d + i) % ND}, device_id_type=MESH
        )
    for i in range(1, NT):
        pl.semaphore_signal(
            barrier, inc=1, device_id={"tm": (me_t + i) % NT}, device_id_type=MESH
        )
    return barrier


def send(axis, size, me, src_of, dst_buf, sems):
    copies = []
    for i in range(1, size):
        peer = (me + i) % size
        copy = pltpu.make_async_remote_copy(
            src_ref=src_of(peer),
            dst_ref=dst_buf.at[me],
            send_sem=sems.at[0, peer],
            recv_sem=sems.at[1, me],
            device_id={axis: peer},
            device_id_type=MESH,
        )
        copy.start()
        copies.append(copy)
    return copies


def arrive(axis, size, me, dst_buf, sems):
    for i in range(1, size):
        peer = (me + i) % size
        pltpu.make_async_remote_copy(
            src_ref=dst_buf.at[peer],
            dst_ref=dst_buf.at[peer],
            send_sem=sems.at[0, peer],
            recv_sem=sems.at[1, peer],
            device_id={axis: peer},
            device_id_type=MESH,
        ).wait_recv()


def trig(ang):
    h = (ang - 32.0) * np.float32(np.pi / 64)
    x = h * h
    s = np.float32(-1 / 39916800)
    for k in (1 / 362880, -1 / 5040, 1 / 120, -1 / 6, 1.0):
        s = s * x + np.float32(k)
    s = s * h
    c = np.float32(1 / 479001600)
    for k in (-1 / 3628800, 1 / 40320, -1 / 720, 1 / 24, -1 / 2, 1.0):
        c = c * x + np.float32(k)
    return 2.0 * s * s - 1.0, -2.0 * s * c


def iota(shape, axis):
    return lax.broadcasted_iota(jnp.int32, shape, axis)


def onehot(index, lanes):
    value = jnp.broadcast_to(index, (lanes, 128)).astype(BF16)
    hit = value == iota((lanes, 128), 0).astype(F32).astype(BF16)
    return jnp.where(hit, jnp.ones_like(value), jnp.zeros_like(value))


def nt(a, b):
    return lax.dot_general(a, b, (((1,), (1,)), ((), ())), preferred_element_type=F32)


def sort_group(group, band_ref, from_row, from_lane):
    before = iota((128, 256), 0)
    lane2 = iota((128, 256), 1)
    upper = jnp.where((lane2 >= 128) | (before < lane2), 1.0, 0.0).astype(BF16)
    bi = iota((128, 128), 0)
    bj = iota((128, 128), 1)
    lower = jnp.where((bi // 8 == bj // 8) & (bj < bi), 1.0, 0.0).astype(BF16)
    r16 = iota((16, 128), 0)
    lane16 = iota((16, 128), 1)
    rows = (r16 % 8).astype(F32).astype(BF16)
    for part in range(GROUP):
        det = group * GROUP + part
        band = band_ref[det]
        hits = [jnp.where(band == b, 1.0, 0.0) for b in range(16)]
        counts = mm(jnp.concatenate(hits, axis=0).astype(BF16), upper)
        total = counts[:, :128] + mm(lower, counts[:, 128:].astype(BF16))
        rank = jnp.zeros((8, 128), F32)
        for b in range(16):
            rank = rank + hits[b] * total[8 * b : 8 * b + 8]
        place = jnp.where(band >= 8, rank + 64.0, rank)
        row = (band % 8).astype(F32)
        left = []
        right = []
        for i in range(8):
            here = jnp.broadcast_to(row[i : i + 1], (16, 128)).astype(BF16) == rows
            digit = jnp.where(r16 < 8, i, lane16).astype(F32).astype(BF16)
            left.append(jnp.where(here, digit, jnp.zeros_like(digit)))
            right.append(onehot(place[i : i + 1], 128))
        source = nt(jnp.concatenate(left, axis=1), jnp.concatenate(right, axis=1))
        from_row[det] = source[:8].astype(jnp.int32)
        from_lane[det] = source[8:].astype(jnp.int32)


def pick(value, det, from_row, from_lane):
    row = from_row[det]
    lane = from_lane[det]
    out = jnp.zeros((8, 128), F32)
    for i in range(8):
        line = jnp.broadcast_to(value[det, i : i + 1, :], (8, 128))
        out = jnp.where(row == i, jnp.take_along_axis(line, lane, axis=1, mode="promise_in_bounds"), out)
    return out


def to_bands(values, outs, from_row, from_lane):
    lane = iota((8, 128), 1)
    for p in range(16):
        for value, out in zip(values, outs):
            u = pick(value, 2 * p, from_row, from_lane)
            v = pick(value, 2 * p + 1, from_row, from_lane)
            out[0:8, p, :] = jnp.where(lane < 64, u, pltpu.roll(v, 64, 1))
            out[8:16, p, :] = jnp.where(lane < 64, pltpu.roll(u, 64, 1), v)


def parts_of(values):
    parts = []
    for v in values:
        hi = v.astype(BF16).astype(F32)
        parts += [hi, v - hi]
    return parts


def map_lines(parts, cell_row):
    rows = iota((16, 128), 0).astype(F32).astype(BF16)
    left = []
    for k in range(16):
        here = jnp.broadcast_to(cell_row[k : k + 1], (16, 128)).astype(BF16) == rows
        lines = []
        for part in parts:
            line = jnp.broadcast_to(part[k : k + 1], (16, 128)).astype(BF16)
            lines.append(jnp.where(here, line, jnp.zeros_like(line)))
        left.append(jnp.concatenate(lines, axis=0))
    return left


def spread(sub0, sub1, count, acc, out):
    both = acc[...].reshape(count, 2, 16, 128)
    both = both[:, 0] + both[:, 1]
    for n in range(NT):
        out[n] = jnp.where(sub0 == n, both[:, :8], 0.0) + jnp.where(sub1 == n, both[:, 8:], 0.0)


def noise_filtering(x, g, ah, al, bh, bl, ch, cl, ih, il, turn):
    count = x.shape[1] // 128
    tc, ts = turn[0], turn[1]
    f = dot3((ah[...], al[...]), split(x))
    rows = []
    for e in range(count):
        re, im = f[:64, 128 * e : 128 * e + 128], f[64:, 128 * e : 128 * e + 128]
        rows.append(jnp.concatenate([re * tc + im * ts, im * tc - re * ts], axis=1))
    f = dot3(split(jnp.concatenate(rows, axis=0)), (bh[...], bl[...]))
    gg = jnp.concatenate([g, g], axis=1)
    f = f * jnp.concatenate([gg] * count, axis=0)
    f = dot3(split(f), (ch[...], cl[...]))
    cols = []
    for e in range(count):
        re, im = f[64 * e : 64 * e + 64, :128], f[64 * e : 64 * e + 64, 128:]
        cols.append(jnp.concatenate([re * tc - im * ts, im * tc + re * ts], axis=0))
    return dot3((ih[...], il[...]), split(jnp.concatenate(cols, axis=1)))


def fused_kernel(
    slots,
    sub,
    *refs,
):
    far, refs = refs[:17], refs[17:]
    out, near, load_sem, refs = refs[0], refs[1:18], refs[18], refs[19:]
    fused_body(slots, sub, far, near, load_sem, out, *refs)


def fused_body(
    slots,
    sub,
    far,
    near,
    load_sem,
    out,
    ybuf,
    yin,
    sbuf,
    xin,
    zbuf,
    zin,
    fbuf,
    fin,
    ftmp,
    obuf,
    cin,
    wt,
    bandt,
    cellt,
    angt,
    cleant,
    from_row,
    from_lane,
    early,
    earlyin,
    late,
    latein,
    wcs,
    rt,
    accc,
    accs,
    tbc,
    tbs,
    ubc,
    ubs,
    sy,
    sx,
    sz,
    sf,
    so,
    se,
    sl,
    tc_sem,
    ts_sem,
):
    me_d = lax.axis_index("det")
    me_t = lax.axis_index("tm")
    loads = []
    for i in range(17):
        load = pltpu.make_async_copy(far[i], near[i], load_sem.at[i])
        load.start()
        loads.append(load)
    barrier = greet(me_d, me_t)
    (tod, weight, w_ref, row_ref, col_ref, ang_ref, gain, couple) = near[:8]
    (ah, al, ih, il, bh, bl, ch, cl, turn) = near[8:]
    loads[0].wait()
    loads[1].wait()
    wsp = split(weight[...])
    for a in range(8):
        x = tod[:, 128 * a : 128 * a + 128]
        ybuf[:, a, :] = dot3(wsp, split(x))
        sbuf[:, a, :] = x
    for load in loads[2:6]:
        load.wait()
    half = iota((32, 128), 1) < 64
    for a in range(8):
        sl_a = slice(128 * a, 128 * a + 128)
        row = row_ref[:, sl_a]
        slot = jnp.where(half, slots[2 * a], slots[2 * a + 1])
        wt[:, a, :] = w_ref[:, sl_a]
        angt[:, a, :] = ang_ref[:, sl_a].astype(F32)
        bandt[:, a, :] = row // 8
        cellt[:, a, :] = ((slot * 8 + row % 8) * 128 + col_ref[:, sl_a]).astype(F32)

    def sort(group, carry):
        sort_group(group, bandt, from_row, from_lane)
        return carry

    lax.fori_loop(CUTS[0], CUTS[1], sort, 0)
    pl.semaphore_wait(barrier, ND - 1 + NT - 1)
    copies = send("det", ND, me_d, lambda p: ybuf.at[pl.ds(2 * p, 2)], yin, sy)
    copies += send("tm", NT, me_t, lambda p: sbuf.at[pl.ds(4 * p, 4)], xin, sx)
    yin[me_d] = ybuf[pl.ds(2 * me_d, 2)]
    xin[me_t] = sbuf[pl.ds(4 * me_t, 4)]
    accc[...] = jnp.zeros_like(accc)
    accs[...] = jnp.zeros_like(accs)
    lax.fori_loop(CUTS[1], CUTS[2], sort, 0)
    arrive("det", ND, me_d, yin, sy)
    z = yin[0]
    for i in range(1, ND):
        z = z + yin[i]
    zbuf[...] = z
    copies += send("tm", NT, me_t, lambda p: zbuf, zin, sz)
    zin[me_t] = z
    to_bands(
        (wt, cellt, angt),
        [early.at[:, i] for i in range(3)],
        from_row,
        from_lane,
    )
    copies += send("det", ND, me_d, lambda p: early.at[p], earlyin, se)
    earlyin[me_d] = early[me_d]
    for load in loads[6:]:
        load.wait()
    g = gain[...]
    gfull = jnp.concatenate([g[:, :64].T, g[:, 64:].T], axis=1)
    arrive("tm", NT, me_t, xin, sx)
    arrive("tm", NT, me_t, zin, sz)
    cols = [jnp.concatenate([xin[m, e] for m in range(NT)], axis=0) for e in range(4)]
    cols += [jnp.concatenate([zin[m, e] for m in range(NT)], axis=0) for e in range(2)]
    f = noise_filtering(
        jnp.concatenate(cols, axis=1), gfull, ah, al, bh, bl, ch, cl, ih, il, turn
    )
    for m in range(NT):
        for e in range(4):
            obuf[m, e] = f[8 * m : 8 * m + 8, 128 * e : 128 * e + 128]
        for e in range(2):
            ftmp[m, e] = f[8 * m : 8 * m + 8, 512 + 128 * e : 640 + 128 * e]
    mine = ftmp[me_t]
    fbuf[...] = mine
    copies += send("det", ND, me_d, lambda p: fbuf, fin, sf)
    copies += send("tm", NT, me_t, lambda p: obuf.at[p], cin, so)
    fin[me_d] = mine
    cin[me_t] = obuf[me_t]
    arrive("det", ND, me_d, earlyin, se)

    def cov_step(step, carry):
        left = []
        right = []
        for i in range(2):
            d = 2 * step + i
            w = earlyin[d, 0]
            cell = earlyin[d, 1].astype(jnp.int32)
            c, s = trig(earlyin[d, 2])
            wc = w * c
            ws = w * s
            cell_row = (cell // 128).astype(F32)
            wcs[d, 0] = wc
            wcs[d, 1] = ws
            wcs[d, 2] = cell_row
            column = (cell % 128).astype(F32)
            for k in range(16):
                hit = onehot(column[k : k + 1], 128)
                rt[d, k] = hit
                right.append(hit)
            left += map_lines(parts_of((w, wc, ws, wc * c, wc * s)), cell_row)
        accc[...] += nt(jnp.concatenate(left, axis=1), jnp.concatenate(right, axis=1))
        return carry

    lax.fori_loop(STEPS[0], STEPS[1], cov_step, 0)
    arrive("det", ND, me_d, fin, sf)
    arrive("tm", NT, me_t, cin, so)
    csp = split(couple[...])
    for a in range(8):
        modes = fin[:, :, a, :].reshape(32, 128)
        cleant[:, a, :] = cin[:, :, a, :].reshape(32, 128) - dot3(csp, split(modes))
    to_bands((cleant,), (late,), from_row, from_lane)
    copies += send("det", ND, me_d, lambda p: late.at[p], latein, sl)
    latein[me_d] = late[me_d]
    sub0 = sub[0, me_t]
    sub1 = sub[1, me_t]
    lax.fori_loop(STEPS[1], STEPS[2], cov_step, 0)
    spread(sub0, sub1, 5, accc, tbc)
    copies += send("tm", NT, me_t, lambda p: tbc.at[p], ubc, tc_sem)
    ubc[me_t] = tbc[me_t]
    arrive("det", ND, me_d, latein, sl)

    def signal_step(step, carry):
        left = []
        right = []
        for i in range(4):
            d = 4 * step + i
            x = latein[d]
            values = (earlyin[d, 0] * x, wcs[d, 0] * x, wcs[d, 1] * x)
            left += map_lines(parts_of(values), wcs[d, 2])
            right += [rt[d, k] for k in range(16)]
        accs[...] += nt(jnp.concatenate(left, axis=1), jnp.concatenate(right, axis=1))
        return carry

    lax.fori_loop(0, ND // 4, signal_step, 0)
    spread(sub0, sub1, 3, accs, tbs)
    final = send("tm", NT, me_t, lambda p: tbs.at[p], ubs, ts_sem)
    ubs[me_t] = tbs[me_t]
    for c in copies:
        c.wait_send()
    arrive("tm", NT, me_t, ubc, tc_sem)
    total = ubc[0]
    for i in range(1, NT):
        total = total + ubc[i]
    out[:5] = total
    arrive("tm", NT, me_t, ubs, ts_sem)
    total = ubs[0]
    for i in range(1, NT):
        total = total + ubs[i]
    out[5:] = total
    for c in final:
        c.wait_send()


def finish_kernel(tot, signal, cov):
    for q in range(3):
        signal[0, q] = tot[5 + q]
    w, wc, ws, wcc, wcs = (tot[q] for q in range(5))
    full = ((w, wc, ws), (wc, wcc, wcs), (ws, wcs, w - wcc))
    for i in range(3):
        for j in range(3):
            cov[0, i, j] = full[i][j]


def body(
    tod,
    noise_filter,
    mode_weight,
    mode_coupling,
    sample_weight,
    pix_row,
    pix_col,
    angle_bin,
    tile_slot,
    slot_submap,
):
    vm = pl.BlockSpec(memory_space=pltpu.VMEM)
    sm = pl.BlockSpec(memory_space=pltpu.SMEM)
    first, last, second, third, turn = dft_tables()
    ah, al = split_const(first)
    ih, il = split_const(last)
    bh, bl = split_const(second)
    ch, cl = split_const(third)
    tables = [jnp.asarray(t) for t in (ah, al, ih, il, bh, bl, ch, cl, turn)]

    def vmem(*shape, dtype=F32):
        return pltpu.VMEM(shape, dtype)

    def sems(size):
        return pltpu.SemaphoreType.DMA((2, size))

    operands = (
        tod,
        mode_weight,
        sample_weight,
        pix_row,
        pix_col,
        angle_bin,
        noise_filter.reshape(64, 128),
        mode_coupling,
        *tables,
    )
    tot = pl.pallas_call(
        fused_kernel,
        out_shape=jax.ShapeDtypeStruct((8, 8, 128), F32),
        in_specs=[sm, sm] + [pl.BlockSpec(memory_space=pl.ANY)] * 17,
        out_specs=vm,
        scratch_shapes=[vmem(*o.shape, dtype=o.dtype) for o in operands]
        + [
            pltpu.SemaphoreType.DMA((17,)),
            vmem(32, 8, 128),
            vmem(ND, 2, 8, 128),
            vmem(32, 8, 128),
            vmem(NT, 4, 8, 128),
            vmem(2, 8, 128),
            vmem(NT, 2, 8, 128),
            vmem(2, 8, 128),
            vmem(ND, 2, 8, 128),
            vmem(NT, 2, 8, 128),
            vmem(NT, 4, 8, 128),
            vmem(NT, 4, 8, 128),
            vmem(32, 8, 128),
            vmem(32, 8, 128, dtype=jnp.int32),
            vmem(32, 8, 128),
            vmem(32, 8, 128),
            vmem(32, 8, 128),
            vmem(32, 8, 128, dtype=jnp.int32),
            vmem(32, 8, 128, dtype=jnp.int32),
            vmem(ND, 3, 16, 128),
            vmem(ND, 3, 16, 128),
            vmem(ND, 16, 128),
            vmem(ND, 16, 128),
            vmem(ND, 3, 16, 128),
            vmem(ND, 16, 128, 128, dtype=BF16),
            vmem(160, 128),
            vmem(96, 128),
            vmem(NT, 5, 8, 128),
            vmem(NT, 3, 8, 128),
            vmem(NT, 5, 8, 128),
            vmem(NT, 3, 8, 128),
            sems(ND),
            sems(NT),
            sems(NT),
            sems(ND),
            sems(NT),
            sems(ND),
            sems(ND),
            sems(NT),
            sems(NT),
        ],
        compiler_params=pltpu.CompilerParams(
            collective_id=0, has_side_effects=True, vmem_limit_bytes=56 << 20
        ),
    )(tile_slot, slot_submap.T, *operands)
    return pl.pallas_call(
        finish_kernel,
        out_shape=(
            jax.ShapeDtypeStruct((1, 3, 8, 128), F32),
            jax.ShapeDtypeStruct((1, 3, 3, 8, 128), F32),
        ),
        in_specs=[vm],
        out_specs=(vm, vm),
    )(tot)


def solution(mesh):
    return jax.shard_map(
        body,
        mesh=mesh,
        in_specs=(
            P("det", "tm"),
            P(),
            P(None, "det"),
            P("det", None),
            P("det", "tm"),
            P("det", "tm"),
            P("det", "tm"),
            P("det", "tm"),
            P("tm"),
            P(),
        ),
        out_specs=(P("tm", None, "det", None), P("tm", None, None, "det", None)),
        check_vma=False,
    )
```

```python
import math

import jax
import jax.numpy as jnp
import numpy as np
from jax import lax
from jax.experimental import pallas as pl
from jax.experimental.pallas import tpu as pltpu
from jax.sharding import PartitionSpec as P

F32 = jnp.float32
BF16 = jnp.bfloat16
MESH = pl.DeviceIdType.MESH
ND = 16
NT = 8
GROUP = 8
CUTS = (0, 1, 4)
STEPS = (0, 6, 8)


def split_const(table):
    hi = table.astype(jnp.bfloat16)
    lo = (table - hi.astype(np.float64)).astype(jnp.bfloat16)
    return hi, lo


def dft_tables():
    one = np.arange(64)
    ang = 2.0 * math.pi * (np.outer(one, one) % 64) / 64
    first = np.concatenate([np.cos(ang), -np.sin(ang)], 0)
    lane = np.arange(128)
    k2 = 2 * (lane % 64) + lane // 64
    ang = 2.0 * math.pi * (np.outer(lane, k2) % 128) / 128
    co, si = np.cos(ang), np.sin(ang)
    second = np.block([[co, -si], [si, co]])
    third = np.block([[co.T, si.T], [-si.T, co.T]])
    ang = 2.0 * math.pi * np.outer(one, lane) / 8192
    turn = np.stack([np.cos(ang), np.sin(ang)]).astype(np.float32)
    return first, first.T / 8192.0, second, third, turn


def split(value):
    hi = value.astype(BF16)
    lo = (value - hi.astype(F32)).astype(BF16)
    return hi, lo


def mm(a, b):
    return lax.dot_general(a, b, (((1,), (0,)), ((), ())), preferred_element_type=F32)


def dot3(a, b):
    return mm(a[0], b[0]) + (mm(a[0], b[1]) + mm(a[1], b[0]))


def greet(me_d, me_t):
    barrier = pltpu.get_barrier_semaphore()
    for i in range(1, ND):
        pl.semaphore_signal(
            barrier, inc=1, device_id={"det": (me_d + i) % ND}, device_id_type=MESH
        )
    for i in range(1, NT):
        pl.semaphore_signal(
            barrier, inc=1, device_id={"tm": (me_t + i) % NT}, device_id_type=MESH
        )
    return barrier


def send(axis, size, me, src_of, dst_buf, sems):
    copies = []
    for i in range(1, size):
        peer = (me + i) % size
        copy = pltpu.make_async_remote_copy(
            src_ref=src_of(peer),
            dst_ref=dst_buf.at[me],
            send_sem=sems.at[0, peer],
            recv_sem=sems.at[1, me],
            device_id={axis: peer},
            device_id_type=MESH,
        )
        copy.start()
        copies.append(copy)
    return copies


def arrive_one(axis, peer, dst_buf, sems):
    pltpu.make_async_remote_copy(
        src_ref=dst_buf.at[peer],
        dst_ref=dst_buf.at[peer],
        send_sem=sems.at[0, peer],
        recv_sem=sems.at[1, peer],
        device_id={axis: peer},
        device_id_type=MESH,
    ).wait_recv()


def arrive(axis, size, me, dst_buf, sems):
    for i in range(1, size):
        arrive_one(axis, (me + i) % size, dst_buf, sems)


def trig(ang):
    h = (ang - 32.0) * np.float32(np.pi / 64)
    x = h * h
    s = np.float32(-1 / 39916800)
    for k in (1 / 362880, -1 / 5040, 1 / 120, -1 / 6, 1.0):
        s = s * x + np.float32(k)
    s = s * h
    c = np.float32(1 / 479001600)
    for k in (-1 / 3628800, 1 / 40320, -1 / 720, 1 / 24, -1 / 2, 1.0):
        c = c * x + np.float32(k)
    return 2.0 * s * s - 1.0, -2.0 * s * c


def iota(shape, axis):
    return lax.broadcasted_iota(jnp.int32, shape, axis)


def onehot(index, lanes):
    value = jnp.broadcast_to(index, (lanes, 128)).astype(BF16)
    hit = value == iota((lanes, 128), 0).astype(F32).astype(BF16)
    return jnp.where(hit, jnp.ones_like(value), jnp.zeros_like(value))


def nt(a, b):
    return lax.dot_general(a, b, (((1,), (1,)), ((), ())), preferred_element_type=F32)


def sort_group(group, band_ref, fields, from_row, from_lane, outs):
    before = iota((128, 256), 0)
    lane2 = iota((128, 256), 1)
    upper = jnp.where((lane2 >= 128) | (before < lane2), 1.0, 0.0).astype(BF16)
    r16 = iota((16, 128), 0)
    lane16 = iota((16, 128), 1)
    lane = iota((8, 128), 1)
    rows = (r16 % 8).astype(F32).astype(BF16)
    w_ref, cell_ref, col_ref, ang_ref = fields
    moved = []
    rank16 = r16.astype(F32).astype(BF16)
    hits = []
    for part in range(GROUP):
        det = group * GROUP + part
        for i in range(8):
            band = jnp.broadcast_to(band_ref[det, i : i + 1, :], (16, 128)).astype(BF16)
            hits.append(jnp.where(band == rank16, jnp.ones_like(band), jnp.zeros_like(band)))
    counts = mm(jnp.concatenate(hits, axis=0), upper)
    for part in range(GROUP):
        det = group * GROUP + part
        row = band_ref[det] % 8.0
        offset = jnp.where(r16 >= 8, 64.0, 0.0)
        places = []
        for i in range(8):
            k = 8 * part + i
            here = counts[16 * k : 16 * k + 16]
            spot = hits[k].astype(F32) * (here[:, :128] + offset)
            places.append(jnp.sum(spot, axis=0, keepdims=True))
            offset = offset + here[:, 128:]
        w = w_ref[det]
        w_hi = w.astype(BF16).astype(F32)
        w_lo = w - w_hi
        cell = cell_ref[det]
        col = col_ref[det]
        ang = ang_ref[det]
        left = []
        right = []
        for i in range(8):
            here = jnp.broadcast_to(row[i : i + 1], (16, 128)).astype(BF16) == rows
            digit = jnp.where(r16 < 8, i, lane16).astype(F32).astype(BF16)
            lines = [digit]
            for u, v in ((w_hi, w_lo), (cell, col), (ang, ang)):
                u = jnp.broadcast_to(u[i : i + 1], (8, 128))
                v = jnp.broadcast_to(v[i : i + 1], (8, 128))
                lines.append(jnp.concatenate([u, v], axis=0).astype(BF16))
            lines = [jnp.where(here, line, jnp.zeros_like(line)) for line in lines]
            left.append(jnp.concatenate(lines, axis=0))
            right.append(onehot(places[i], 128))
        source = nt(jnp.concatenate(left, axis=1), jnp.concatenate(right, axis=1))
        from_row[det] = source[:8].astype(jnp.int32)
        from_lane[det] = source[8:16].astype(jnp.int32)
        moved.append(
            (
                source[16:24] + source[24:32],
                source[32:40] * 128.0 + source[40:48],
                source[48:56],
            )
        )
    for k in range(GROUP // 2):
        p = group * (GROUP // 2) + k
        for i in range(3):
            u, v = moved[2 * k][i], moved[2 * k + 1][i]
            low = jnp.where(lane < 64, u, pltpu.roll(v, 64, 1))
            high = jnp.where(lane < 64, pltpu.roll(u, 64, 1), v)
            outs[0:8, i, pl.ds(p, 1), :] = low.reshape(8, 1, 128)
            outs[8:16, i, pl.ds(p, 1), :] = high.reshape(8, 1, 128)


def pick(value, det, from_row, from_lane):
    row = from_row[det]
    lane = from_lane[det]
    out = jnp.zeros((8, 128), F32)
    for i in range(8):
        line = jnp.broadcast_to(value[det, i : i + 1, :], (8, 128))
        out = jnp.where(row == i, jnp.take_along_axis(line, lane, axis=1, mode="promise_in_bounds"), out)
    return out


def to_bands(values, outs, from_row, from_lane):
    lane = iota((8, 128), 1)
    for p in range(16):
        for value, out in zip(values, outs):
            u = pick(value, 2 * p, from_row, from_lane)
            v = pick(value, 2 * p + 1, from_row, from_lane)
            out[0:8, p, :] = jnp.where(lane < 64, u, pltpu.roll(v, 64, 1))
            out[8:16, p, :] = jnp.where(lane < 64, pltpu.roll(u, 64, 1), v)


def parts_of(values):
    parts = []
    for v in values:
        hi = v.astype(BF16).astype(F32)
        parts += [hi, v - hi]
    return parts


def map_lines(parts, cell_row):
    rows = iota((16, 128), 0).astype(F32).astype(BF16)
    left = []
    for k in range(16):
        here = jnp.broadcast_to(cell_row[k : k + 1], (16, 128)).astype(BF16) == rows
        lines = []
        for part in parts:
            line = jnp.broadcast_to(part[k : k + 1], (16, 128)).astype(BF16)
            lines.append(jnp.where(here, line, jnp.zeros_like(line)))
        left.append(jnp.concatenate(lines, axis=0))
    return left


def spread(sub0, sub1, count, acc, out):
    both = acc[...].reshape(count, 2, 16, 128)
    both = both[:, 0] + both[:, 1]
    for n in range(NT):
        out[n] = jnp.where(sub0 == n, both[:, :8], 0.0) + jnp.where(sub1 == n, both[:, 8:], 0.0)


def noise_filtering(x, g, ah, al, bh, bl, ch, cl, ih, il, turn):
    count = x.shape[1] // 128
    tc, ts = turn[0], turn[1]
    f = dot3((ah[...], al[...]), split(x))
    rows = []
    for e in range(count):
        re, im = f[:64, 128 * e : 128 * e + 128], f[64:, 128 * e : 128 * e + 128]
        rows.append(jnp.concatenate([re * tc + im * ts, im * tc - re * ts], axis=1))
    f = dot3(split(jnp.concatenate(rows, axis=0)), (bh[...], bl[...]))
    gg = jnp.concatenate([g, g], axis=1)
    f = f * jnp.concatenate([gg] * count, axis=0)
    f = dot3(split(f), (ch[...], cl[...]))
    cols = []
    for e in range(count):
        re, im = f[64 * e : 64 * e + 64, :128], f[64 * e : 64 * e + 64, 128:]
        cols.append(jnp.concatenate([re * tc - im * ts, im * tc + re * ts], axis=0))
    return dot3((ih[...], il[...]), split(jnp.concatenate(cols, axis=1)))


def fused_kernel(
    slots,
    sub,
    *refs,
):
    far, refs = refs[:17], refs[17:]
    out, near, load_sem, refs = refs[0], refs[1:18], refs[18], refs[19:]
    fused_body(slots, sub, far, near, load_sem, out, *refs)


def fused_body(
    slots,
    sub,
    far,
    near,
    load_sem,
    out,
    ybuf,
    yin,
    sbuf,
    xin,
    zbuf,
    zin,
    fbuf,
    fin,
    ftmp,
    obuf,
    cin,
    wt,
    bandt,
    cellt,
    colt,
    angt,
    cleant,
    from_row,
    from_lane,
    early,
    earlyin,
    late,
    latein,
    wcs,
    rt,
    accc,
    accs,
    tbc,
    tbs,
    ubc,
    ubs,
    sy,
    sx,
    sz,
    sf,
    so,
    se,
    sl,
    tc_sem,
    ts_sem,
):
    me_d = lax.axis_index("det")
    me_t = lax.axis_index("tm")
    loads = []
    for i in range(17):
        load = pltpu.make_async_copy(far[i], near[i], load_sem.at[i])
        load.start()
        loads.append(load)
    barrier = greet(me_d, me_t)
    (tod, weight, w_ref, row_ref, col_ref, ang_ref, gain, couple) = near[:8]
    (ah, al, ih, il, bh, bl, ch, cl, turn) = near[8:]
    loads[0].wait()
    loads[1].wait()
    wsp = split(weight[...])
    for a in range(8):
        x = tod[:, 128 * a : 128 * a + 128]
        ybuf[:, a, :] = dot3(wsp, split(x))
        sbuf[:, a, :] = x
    for load in loads[2:6]:
        load.wait()
    half = iota((32, 128), 1) < 64
    for a in range(8):
        sl_a = slice(128 * a, 128 * a + 128)
        row = row_ref[:, sl_a]
        slot = jnp.where(half, slots[2 * a], slots[2 * a + 1])
        wt[:, a, :] = w_ref[:, sl_a]
        angt[:, a, :] = ang_ref[:, sl_a].astype(F32)
        bandt[:, a, :] = (row // 8).astype(F32)
        cellt[:, a, :] = (slot * 8 + row % 8).astype(F32)
        colt[:, a, :] = col_ref[:, sl_a].astype(F32)

    def sort(group, carry):
        sort_group(group, bandt, (wt, cellt, colt, angt), from_row, from_lane, early)
        return carry

    lax.fori_loop(CUTS[0], CUTS[1], sort, 0)
    pl.semaphore_wait(barrier, ND - 1 + NT - 1)
    copies = send("det", ND, me_d, lambda p: ybuf.at[pl.ds(2 * p, 2)], yin, sy)
    copies += send("tm", NT, me_t, lambda p: sbuf.at[pl.ds(4 * p, 4)], xin, sx)
    yin[me_d] = ybuf[pl.ds(2 * me_d, 2)]
    xin[me_t] = sbuf[pl.ds(4 * me_t, 4)]
    accc[...] = jnp.zeros_like(accc)
    accs[...] = jnp.zeros_like(accs)
    lax.fori_loop(CUTS[1], CUTS[2], sort, 0)
    copies += send("det", ND, me_d, lambda p: early.at[p], earlyin, se)
    earlyin[me_d] = early[me_d]
    arrive("det", ND, me_d, yin, sy)
    z = yin[0]
    for i in range(1, ND):
        z = z + yin[i]
    zbuf[...] = z
    copies += send("tm", NT, me_t, lambda p: zbuf, zin, sz)
    zin[me_t] = z
    for load in loads[6:]:
        load.wait()
    g = gain[...]
    gfull = jnp.concatenate([g[:, :64].T, g[:, 64:].T], axis=1)
    arrive("tm", NT, me_t, xin, sx)
    arrive("tm", NT, me_t, zin, sz)
    cols = [jnp.concatenate([xin[m, e] for m in range(NT)], axis=0) for e in range(4)]
    cols += [jnp.concatenate([zin[m, e] for m in range(NT)], axis=0) for e in range(2)]
    f = noise_filtering(
        jnp.concatenate(cols, axis=1), gfull, ah, al, bh, bl, ch, cl, ih, il, turn
    )
    for m in range(NT):
        for e in range(4):
            obuf[m, e] = f[8 * m : 8 * m + 8, 128 * e : 128 * e + 128]
        for e in range(2):
            ftmp[m, e] = f[8 * m : 8 * m + 8, 512 + 128 * e : 640 + 128 * e]
    mine = ftmp[me_t]
    fbuf[...] = mine
    copies += send("det", ND, me_d, lambda p: fbuf, fin, sf)
    copies += send("tm", NT, me_t, lambda p: obuf.at[p], cin, so)
    fin[me_d] = mine
    cin[me_t] = obuf[me_t]
    arrive("det", ND, me_d, earlyin, se)

    def cov_step(step, carry):
        left = []
        right = []
        for i in range(2):
            d = 2 * step + i
            w = earlyin[d, 0]
            cell = earlyin[d, 1].astype(jnp.int32)
            c, s = trig(earlyin[d, 2])
            wc = w * c
            ws = w * s
            cell_row = (cell // 128).astype(F32)
            wcs[d, 0] = wc
            wcs[d, 1] = ws
            wcs[d, 2] = cell_row
            column = (cell % 128).astype(F32)
            for k in range(16):
                hit = onehot(column[k : k + 1], 128)
                rt[d, k] = hit
                right.append(hit)
            left += map_lines(parts_of((w, wc, ws, wc * c, wc * s)), cell_row)
        accc[...] += nt(jnp.concatenate(left, axis=1), jnp.concatenate(right, axis=1))
        return carry

    lax.fori_loop(STEPS[0], STEPS[1], cov_step, 0)
    arrive("det", ND, me_d, fin, sf)
    arrive("tm", NT, me_t, cin, so)
    csp = split(couple[...])
    for a in range(8):
        modes = fin[:, :, a, :].reshape(32, 128)
        cleant[:, a, :] = cin[:, :, a, :].reshape(32, 128) - dot3(csp, split(modes))
    to_bands((cleant,), (late,), from_row, from_lane)
    copies += send("det", ND, me_d, lambda p: late.at[p], latein, sl)
    latein[me_d] = late[me_d]
    sub0 = sub[0, me_t]
    sub1 = sub[1, me_t]
    lax.fori_loop(STEPS[1], STEPS[2], cov_step, 0)
    spread(sub0, sub1, 5, accc, tbc)
    copies += send("tm", NT, me_t, lambda p: tbc.at[p], ubc, tc_sem)
    ubc[me_t] = tbc[me_t]
    def signal_step(step, carry):
        dz = step + step // 2 - 2 * (step // 3)
        row = (me_d // 4 + dz) % 4 * 4
        left = []
        right = []

        @pl.when(step > 0)
        def _():
            arrive_one("det", row + me_d % 4, latein, sl)

        for dx in (1, 3, 2):
            arrive_one("det", row + (me_d + dx) % 4, latein, sl)
        for dx in range(4):
            d = row + (me_d + dx) % 4
            x = latein[d]
            values = (earlyin[d, 0] * x, wcs[d, 0] * x, wcs[d, 1] * x)
            left += map_lines(parts_of(values), wcs[d, 2])
            right += [rt[d, k] for k in range(16)]
        accs[...] += nt(jnp.concatenate(left, axis=1), jnp.concatenate(right, axis=1))
        return carry

    lax.fori_loop(0, 4, signal_step, 0)
    spread(sub0, sub1, 3, accs, tbs)
    final = send("tm", NT, me_t, lambda p: tbs.at[p], ubs, ts_sem)
    ubs[me_t] = tbs[me_t]
    for c in copies:
        c.wait_send()
    arrive("tm", NT, me_t, ubc, tc_sem)
    total = ubc[0]
    for i in range(1, NT):
        total = total + ubc[i]
    out[:5] = total
    arrive("tm", NT, me_t, ubs, ts_sem)
    total = ubs[0]
    for i in range(1, NT):
        total = total + ubs[i]
    out[5:] = total
    for c in final:
        c.wait_send()


def finish_kernel(tot, signal, cov):
    for q in range(3):
        signal[0, q] = tot[5 + q]
    w, wc, ws, wcc, wcs = (tot[q] for q in range(5))
    full = ((w, wc, ws), (wc, wcc, wcs), (ws, wcs, w - wcc))
    for i in range(3):
        for j in range(3):
            cov[0, i, j] = full[i][j]


def body(
    tod,
    noise_filter,
    mode_weight,
    mode_coupling,
    sample_weight,
    pix_row,
    pix_col,
    angle_bin,
    tile_slot,
    slot_submap,
):
    vm = pl.BlockSpec(memory_space=pltpu.VMEM)
    sm = pl.BlockSpec(memory_space=pltpu.SMEM)
    first, last, second, third, turn = dft_tables()
    ah, al = split_const(first)
    ih, il = split_const(last)
    bh, bl = split_const(second)
    ch, cl = split_const(third)
    tables = [jnp.asarray(t) for t in (ah, al, ih, il, bh, bl, ch, cl, turn)]

    def vmem(*shape, dtype=F32):
        return pltpu.VMEM(shape, dtype)

    def sems(size):
        return pltpu.SemaphoreType.DMA((2, size))

    operands = (
        tod,
        mode_weight,
        sample_weight,
        pix_row,
        pix_col,
        angle_bin,
        noise_filter.reshape(64, 128),
        mode_coupling,
        *tables,
    )
    tot = pl.pallas_call(
        fused_kernel,
        out_shape=jax.ShapeDtypeStruct((8, 8, 128), F32),
        in_specs=[sm, sm] + [pl.BlockSpec(memory_space=pl.ANY)] * 17,
        out_specs=vm,
        scratch_shapes=[vmem(*o.shape, dtype=o.dtype) for o in operands]
        + [
            pltpu.SemaphoreType.DMA((17,)),
            vmem(32, 8, 128),
            vmem(ND, 2, 8, 128),
            vmem(32, 8, 128),
            vmem(NT, 4, 8, 128),
            vmem(2, 8, 128),
            vmem(NT, 2, 8, 128),
            vmem(2, 8, 128),
            vmem(ND, 2, 8, 128),
            vmem(NT, 2, 8, 128),
            vmem(NT, 4, 8, 128),
            vmem(NT, 4, 8, 128),
            vmem(32, 8, 128),
            vmem(32, 8, 128),
            vmem(32, 8, 128),
            vmem(32, 8, 128),
            vmem(32, 8, 128),
            vmem(32, 8, 128),
            vmem(32, 8, 128, dtype=jnp.int32),
            vmem(32, 8, 128, dtype=jnp.int32),
            vmem(ND, 3, 16, 128),
            vmem(ND, 3, 16, 128),
            vmem(ND, 16, 128),
            vmem(ND, 16, 128),
            vmem(ND, 3, 16, 128),
            vmem(ND, 16, 128, 128, dtype=BF16),
            vmem(160, 128),
            vmem(96, 128),
            vmem(NT, 5, 8, 128),
            vmem(NT, 3, 8, 128),
            vmem(NT, 5, 8, 128),
            vmem(NT, 3, 8, 128),
            sems(ND),
            sems(NT),
            sems(NT),
            sems(ND),
            sems(NT),
            sems(ND),
            sems(ND),
            sems(NT),
            sems(NT),
        ],
        compiler_params=pltpu.CompilerParams(
            collective_id=0, has_side_effects=True, vmem_limit_bytes=56 << 20
        ),
    )(tile_slot, slot_submap.T, *operands)
    return pl.pallas_call(
        finish_kernel,
        out_shape=(
            jax.ShapeDtypeStruct((1, 3, 8, 128), F32),
            jax.ShapeDtypeStruct((1, 3, 3, 8, 128), F32),
        ),
        in_specs=[vm],
        out_specs=(vm, vm),
    )(tot)


def solution(mesh):
    return jax.shard_map(
        body,
        mesh=mesh,
        in_specs=(
            P("det", "tm"),
            P(),
            P(None, "det"),
            P("det", None),
            P("det", "tm"),
            P("det", "tm"),
            P("det", "tm"),
            P("det", "tm"),
            P("tm"),
            P(),
        ),
        out_specs=(P("tm", None, "det", None), P("tm", None, None, "det", None)),
        check_vma=False,
    )
```

```python
import math

import jax
import jax.numpy as jnp
import numpy as np
from jax import lax
from jax.experimental import pallas as pl
from jax.experimental.pallas import tpu as pltpu
from jax.sharding import PartitionSpec as P

F32 = jnp.float32
BF16 = jnp.bfloat16
MESH = pl.DeviceIdType.MESH
ND = 16
NT = 8
GROUP = 8
CUTS = (0, 1, 4)
STEPS = (0, 6, 8)


def split_const(table):
    hi = table.astype(jnp.bfloat16)
    lo = (table - hi.astype(np.float64)).astype(jnp.bfloat16)
    return hi, lo


def dft_tables():
    one = np.arange(64)
    ang = 2.0 * math.pi * (np.outer(one, one) % 64) / 64
    first = np.concatenate([np.cos(ang), -np.sin(ang)], 0)
    lane = np.arange(128)
    k2 = 2 * (lane % 64) + lane // 64
    ang = 2.0 * math.pi * (np.outer(lane, k2) % 128) / 128
    co, si = np.cos(ang), np.sin(ang)
    second = np.block([[co, -si], [si, co]])
    third = np.block([[co.T, si.T], [-si.T, co.T]])
    ang = 2.0 * math.pi * np.outer(one, lane) / 8192
    turn = np.stack([np.cos(ang), np.sin(ang)]).astype(np.float32)
    return first, first.T / 8192.0, second, third, turn


def split(value):
    hi = value.astype(BF16)
    lo = (value - hi.astype(F32)).astype(BF16)
    return hi, lo


def mm(a, b):
    return lax.dot_general(a, b, (((1,), (0,)), ((), ())), preferred_element_type=F32)


def dot3(a, b):
    return mm(a[0], b[0]) + (mm(a[0], b[1]) + mm(a[1], b[0]))


def peers(axis, me):
    if axis == "tm":
        return [(me + i) % NT for i in (4, 5, 3, 2, 6, 7, 1)]
    steps = ((dz, dx) for dz in range(4) for dx in range(4) if dz or dx)
    steps = sorted(steps, key=lambda o: -(min(o[0], 4 - o[0]) + min(o[1], 4 - o[1])))
    return [(me // 4 + dz) % 4 * 4 + (me + dx) % 4 for dz, dx in steps]


def greet(me_d, me_t):
    barrier = pltpu.get_barrier_semaphore()
    for axis, me in (("det", me_d), ("tm", me_t)):
        for peer in peers(axis, me):
            pl.semaphore_signal(
                barrier, inc=1, device_id={axis: peer}, device_id_type=MESH
            )
    return barrier


def send(axis, size, me, src_of, dst_buf, sems):
    copies = []
    for peer in peers(axis, me):
        copy = pltpu.make_async_remote_copy(
            src_ref=src_of(peer),
            dst_ref=dst_buf.at[me],
            send_sem=sems.at[0, peer],
            recv_sem=sems.at[1, me],
            device_id={axis: peer},
            device_id_type=MESH,
        )
        copy.start()
        copies.append(copy)
    return copies


def arrive_one(axis, peer, dst_buf, sems):
    pltpu.make_async_remote_copy(
        src_ref=dst_buf.at[peer],
        dst_ref=dst_buf.at[peer],
        send_sem=sems.at[0, peer],
        recv_sem=sems.at[1, peer],
        device_id={axis: peer},
        device_id_type=MESH,
    ).wait_recv()


def arrive(axis, size, me, dst_buf, sems):
    for i in range(1, size):
        arrive_one(axis, (me + i) % size, dst_buf, sems)


def trig(ang):
    h = (ang - 32.0) * np.float32(np.pi / 64)
    x = h * h
    s = np.float32(-1 / 39916800)
    for k in (1 / 362880, -1 / 5040, 1 / 120, -1 / 6, 1.0):
        s = s * x + np.float32(k)
    s = s * h
    c = np.float32(1 / 479001600)
    for k in (-1 / 3628800, 1 / 40320, -1 / 720, 1 / 24, -1 / 2, 1.0):
        c = c * x + np.float32(k)
    return 2.0 * s * s - 1.0, -2.0 * s * c


def iota(shape, axis):
    return lax.broadcasted_iota(jnp.int32, shape, axis)


def onehot(index, lanes):
    value = jnp.broadcast_to(index, (lanes, 128)).astype(BF16)
    hit = value == iota((lanes, 128), 0).astype(F32).astype(BF16)
    return jnp.where(hit, jnp.ones_like(value), jnp.zeros_like(value))


def nt(a, b):
    return lax.dot_general(a, b, (((1,), (1,)), ((), ())), preferred_element_type=F32)


def sort_group(group, band_ref, fields, from_row, from_lane, outs):
    before = iota((128, 256), 0)
    lane2 = iota((128, 256), 1)
    upper = jnp.where((lane2 >= 128) | (before < lane2), 1.0, 0.0).astype(BF16)
    r16 = iota((16, 128), 0)
    lane16 = iota((16, 128), 1)
    lane = iota((8, 128), 1)
    rows = (r16 % 8).astype(F32).astype(BF16)
    w_ref, cell_ref, col_ref, ang_ref = fields
    moved = []
    rank16 = r16.astype(F32).astype(BF16)
    hits = []
    for part in range(GROUP):
        det = group * GROUP + part
        for i in range(8):
            band = jnp.broadcast_to(band_ref[det, i : i + 1, :], (16, 128)).astype(BF16)
            hits.append(jnp.where(band == rank16, jnp.ones_like(band), jnp.zeros_like(band)))
    counts = mm(jnp.concatenate(hits, axis=0), upper)
    for part in range(GROUP):
        det = group * GROUP + part
        row = band_ref[det] % 8.0
        offset = jnp.where(r16 >= 8, 64.0, 0.0)
        places = []
        for i in range(8):
            k = 8 * part + i
            here = counts[16 * k : 16 * k + 16]
            spot = hits[k].astype(F32) * (here[:, :128] + offset)
            places.append(jnp.sum(spot, axis=0, keepdims=True))
            offset = offset + here[:, 128:]
        w = w_ref[det]
        w_hi = w.astype(BF16).astype(F32)
        w_lo = w - w_hi
        cell = cell_ref[det]
        col = col_ref[det]
        ang = ang_ref[det]
        left = []
        right = []
        for i in range(8):
            here = jnp.broadcast_to(row[i : i + 1], (16, 128)).astype(BF16) == rows
            digit = jnp.where(r16 < 8, i, lane16).astype(F32).astype(BF16)
            lines = [digit]
            for u, v in ((w_hi, w_lo), (cell, col), (ang, ang)):
                u = jnp.broadcast_to(u[i : i + 1], (8, 128))
                v = jnp.broadcast_to(v[i : i + 1], (8, 128))
                lines.append(jnp.concatenate([u, v], axis=0).astype(BF16))
            lines = [jnp.where(here, line, jnp.zeros_like(line)) for line in lines]
            left.append(jnp.concatenate(lines, axis=0))
            right.append(onehot(places[i], 128))
        source = nt(jnp.concatenate(left, axis=1), jnp.concatenate(right, axis=1))
        from_row[det] = source[:8].astype(jnp.int32)
        from_lane[det] = source[8:16].astype(jnp.int32)
        moved.append(
            (
                source[16:24] + source[24:32],
                source[32:40] * 128.0 + source[40:48],
                source[48:56],
            )
        )
    for k in range(GROUP // 2):
        p = group * (GROUP // 2) + k
        for i in range(3):
            u, v = moved[2 * k][i], moved[2 * k + 1][i]
            low = jnp.where(lane < 64, u, pltpu.roll(v, 64, 1))
            high = jnp.where(lane < 64, pltpu.roll(u, 64, 1), v)
            outs[0:8, i, pl.ds(p, 1), :] = low.reshape(8, 1, 128)
            outs[8:16, i, pl.ds(p, 1), :] = high.reshape(8, 1, 128)


def pick(value, det, from_row, from_lane):
    row = from_row[det]
    lane = from_lane[det]
    out = jnp.zeros((8, 128), F32)
    for i in range(8):
        line = jnp.broadcast_to(value[det, i : i + 1, :], (8, 128))
        out = jnp.where(row == i, jnp.take_along_axis(line, lane, axis=1, mode="promise_in_bounds"), out)
    return out


def to_bands(values, outs, from_row, from_lane):
    lane = iota((8, 128), 1)
    for p in range(16):
        for value, out in zip(values, outs):
            u = pick(value, 2 * p, from_row, from_lane)
            v = pick(value, 2 * p + 1, from_row, from_lane)
            out[0:8, p, :] = jnp.where(lane < 64, u, pltpu.roll(v, 64, 1))
            out[8:16, p, :] = jnp.where(lane < 64, pltpu.roll(u, 64, 1), v)


def parts_of(values):
    parts = []
    for v in values:
        hi = v.astype(BF16).astype(F32)
        parts += [hi, v - hi]
    return parts


def map_lines(parts, cell_row):
    rows = iota((16, 128), 0).astype(F32).astype(BF16)
    left = []
    for k in range(16):
        here = jnp.broadcast_to(cell_row[k : k + 1], (16, 128)).astype(BF16) == rows
        lines = []
        for part in parts:
            line = jnp.broadcast_to(part[k : k + 1], (16, 128)).astype(BF16)
            lines.append(jnp.where(here, line, jnp.zeros_like(line)))
        left.append(jnp.concatenate(lines, axis=0))
    return left


def spread(sub0, sub1, count, acc, out):
    both = acc[...].reshape(count, 2, 16, 128)
    both = both[:, 0] + both[:, 1]
    for n in range(NT):
        out[n] = jnp.where(sub0 == n, both[:, :8], 0.0) + jnp.where(sub1 == n, both[:, 8:], 0.0)


def noise_filtering(x, g, ah, al, bh, bl, ch, cl, ih, il, turn):
    count = x.shape[1] // 128
    tc, ts = turn[0], turn[1]
    f = dot3((ah[...], al[...]), split(x))
    rows = []
    for e in range(count):
        re, im = f[:64, 128 * e : 128 * e + 128], f[64:, 128 * e : 128 * e + 128]
        rows.append(jnp.concatenate([re * tc + im * ts, im * tc - re * ts], axis=1))
    f = dot3(split(jnp.concatenate(rows, axis=0)), (bh[...], bl[...]))
    gg = jnp.concatenate([g, g], axis=1)
    f = f * jnp.concatenate([gg] * count, axis=0)
    f = dot3(split(f), (ch[...], cl[...]))
    cols = []
    for e in range(count):
        re, im = f[64 * e : 64 * e + 64, :128], f[64 * e : 64 * e + 64, 128:]
        cols.append(jnp.concatenate([re * tc - im * ts, im * tc + re * ts], axis=0))
    return dot3((ih[...], il[...]), split(jnp.concatenate(cols, axis=1)))


def fused_kernel(
    slots,
    sub,
    *refs,
):
    far, refs = refs[:17], refs[17:]
    out, near, load_sem, refs = refs[0], refs[1:18], refs[18], refs[19:]
    fused_body(slots, sub, far, near, load_sem, out, *refs)


def fused_body(
    slots,
    sub,
    far,
    near,
    load_sem,
    out,
    ybuf,
    yin,
    sbuf,
    xin,
    zbuf,
    zin,
    fbuf,
    fin,
    ftmp,
    obuf,
    cin,
    wt,
    bandt,
    cellt,
    colt,
    angt,
    cleant,
    from_row,
    from_lane,
    early,
    earlyin,
    late,
    latein,
    wcs,
    rt,
    accc,
    accs,
    tbc,
    tbs,
    ubc,
    ubs,
    sy,
    sx,
    sz,
    sf,
    so,
    se,
    sl,
    tc_sem,
    ts_sem,
):
    me_d = lax.axis_index("det")
    me_t = lax.axis_index("tm")
    barrier = greet(me_d, me_t)
    loads = []
    for i in range(17):
        load = pltpu.make_async_copy(far[i], near[i], load_sem.at[i])
        load.start()
        loads.append(load)
    (tod, weight, w_ref, row_ref, col_ref, ang_ref, gain, couple) = near[:8]
    (ah, al, ih, il, bh, bl, ch, cl, turn) = near[8:]
    loads[0].wait()
    loads[1].wait()
    wsp = split(weight[...])
    for a in range(8):
        x = tod[:, 128 * a : 128 * a + 128]
        ybuf[:, a, :] = dot3(wsp, split(x))
        sbuf[:, a, :] = x
    for load in loads[2:6]:
        load.wait()
    half = iota((32, 128), 1) < 64
    for a in range(8):
        sl_a = slice(128 * a, 128 * a + 128)
        row = row_ref[:, sl_a]
        slot = jnp.where(half, slots[2 * a], slots[2 * a + 1])
        wt[:, a, :] = w_ref[:, sl_a]
        angt[:, a, :] = ang_ref[:, sl_a].astype(F32)
        bandt[:, a, :] = (row // 8).astype(F32)
        cellt[:, a, :] = (slot * 8 + row % 8).astype(F32)
        colt[:, a, :] = col_ref[:, sl_a].astype(F32)

    def sort(group, carry):
        sort_group(group, bandt, (wt, cellt, colt, angt), from_row, from_lane, early)
        return carry

    lax.fori_loop(CUTS[0], CUTS[1], sort, 0)
    pl.semaphore_wait(barrier, ND - 1 + NT - 1)
    copies = send("det", ND, me_d, lambda p: ybuf.at[pl.ds(2 * p, 2)], yin, sy)
    copies += send("tm", NT, me_t, lambda p: sbuf.at[pl.ds(4 * p, 4)], xin, sx)
    yin[me_d] = ybuf[pl.ds(2 * me_d, 2)]
    xin[me_t] = sbuf[pl.ds(4 * me_t, 4)]
    accc[...] = jnp.zeros_like(accc)
    accs[...] = jnp.zeros_like(accs)
    lax.fori_loop(CUTS[1], CUTS[2], sort, 0)
    copies += send("det", ND, me_d, lambda p: early.at[p], earlyin, se)
    earlyin[me_d] = early[me_d]
    arrive("det", ND, me_d, yin, sy)
    z = yin[0]
    for i in range(1, ND):
        z = z + yin[i]
    zbuf[...] = z
    copies += send("tm", NT, me_t, lambda p: zbuf, zin, sz)
    zin[me_t] = z
    for load in loads[6:]:
        load.wait()
    g = gain[...]
    gfull = jnp.concatenate([g[:, :64].T, g[:, 64:].T], axis=1)
    arrive("tm", NT, me_t, xin, sx)
    filt = (gfull, ah, al, bh, bl, ch, cl, ih, il, turn)
    cols = [jnp.concatenate([xin[m, e] for m in range(NT)], axis=0) for e in range(4)]
    f = noise_filtering(jnp.concatenate(cols, axis=1), *filt)
    for m in range(NT):
        for e in range(4):
            obuf[m, e] = f[8 * m : 8 * m + 8, 128 * e : 128 * e + 128]
    copies += send("tm", NT, me_t, lambda p: obuf.at[p], cin, so)
    cin[me_t] = obuf[me_t]
    arrive("tm", NT, me_t, zin, sz)
    cols = [jnp.concatenate([zin[m, e] for m in range(NT)], axis=0) for e in range(2)]
    f = noise_filtering(jnp.concatenate(cols, axis=1), *filt)
    for m in range(NT):
        for e in range(2):
            ftmp[m, e] = f[8 * m : 8 * m + 8, 128 * e : 128 * e + 128]
    mine = ftmp[me_t]
    fbuf[...] = mine
    copies += send("det", ND, me_d, lambda p: fbuf, fin, sf)
    fin[me_d] = mine
    arrive("det", ND, me_d, earlyin, se)

    def cov_step(step, carry):
        left = []
        right = []
        for i in range(2):
            d = 2 * step + i
            w = earlyin[d, 0]
            cell = earlyin[d, 1].astype(jnp.int32)
            c, s = trig(earlyin[d, 2])
            wc = w * c
            ws = w * s
            cell_row = (cell // 128).astype(F32)
            wcs[d, 0] = wc
            wcs[d, 1] = ws
            wcs[d, 2] = cell_row
            column = (cell % 128).astype(F32)
            for k in range(16):
                hit = onehot(column[k : k + 1], 128)
                rt[d, k] = hit
                right.append(hit)
            left += map_lines(parts_of((w, wc, ws, wc * c, wc * s)), cell_row)
        accc[...] += nt(jnp.concatenate(left, axis=1), jnp.concatenate(right, axis=1))
        return carry

    lax.fori_loop(STEPS[0], STEPS[1], cov_step, 0)
    arrive("det", ND, me_d, fin, sf)
    arrive("tm", NT, me_t, cin, so)
    csp = split(couple[...])
    for a in range(8):
        modes = fin[:, :, a, :].reshape(32, 128)
        cleant[:, a, :] = cin[:, :, a, :].reshape(32, 128) - dot3(csp, split(modes))
    to_bands((cleant,), (late,), from_row, from_lane)
    copies += send("det", ND, me_d, lambda p: late.at[p], latein, sl)
    latein[me_d] = late[me_d]
    sub0 = sub[0, me_t]
    sub1 = sub[1, me_t]
    lax.fori_loop(STEPS[1], STEPS[2], cov_step, 0)
    spread(sub0, sub1, 5, accc, tbc)
    copies += send("tm", NT, me_t, lambda p: tbc.at[p], ubc, tc_sem)
    ubc[me_t] = tbc[me_t]
    def signal_step(step, carry):
        dz = step + step // 2 - 2 * (step // 3)
        row = (me_d // 4 + dz) % 4 * 4
        left = []
        right = []

        @pl.when(step > 0)
        def _():
            arrive_one("det", row + me_d % 4, latein, sl)

        for dx in (1, 3, 2):
            arrive_one("det", row + (me_d + dx) % 4, latein, sl)
        for dx in range(4):
            d = row + (me_d + dx) % 4
            x = latein[d]
            values = (earlyin[d, 0] * x, wcs[d, 0] * x, wcs[d, 1] * x)
            left += map_lines(parts_of(values), wcs[d, 2])
            right += [rt[d, k] for k in range(16)]
        accs[...] += nt(jnp.concatenate(left, axis=1), jnp.concatenate(right, axis=1))
        return carry

    lax.fori_loop(0, 4, signal_step, 0)
    spread(sub0, sub1, 3, accs, tbs)
    final = send("tm", NT, me_t, lambda p: tbs.at[p], ubs, ts_sem)
    ubs[me_t] = tbs[me_t]
    for c in copies:
        c.wait_send()
    arrive("tm", NT, me_t, ubc, tc_sem)
    total = ubc[0]
    for i in range(1, NT):
        total = total + ubc[i]
    out[:5] = total
    arrive("tm", NT, me_t, ubs, ts_sem)
    total = ubs[0]
    for i in range(1, NT):
        total = total + ubs[i]
    out[5:] = total
    for c in final:
        c.wait_send()


def finish_kernel(tot, signal, cov):
    for q in range(3):
        signal[0, q] = tot[5 + q]
    w, wc, ws, wcc, wcs = (tot[q] for q in range(5))
    full = ((w, wc, ws), (wc, wcc, wcs), (ws, wcs, w - wcc))
    for i in range(3):
        for j in range(3):
            cov[0, i, j] = full[i][j]


def body(
    tod,
    noise_filter,
    mode_weight,
    mode_coupling,
    sample_weight,
    pix_row,
    pix_col,
    angle_bin,
    tile_slot,
    slot_submap,
):
    vm = pl.BlockSpec(memory_space=pltpu.VMEM)
    sm = pl.BlockSpec(memory_space=pltpu.SMEM)
    first, last, second, third, turn = dft_tables()
    ah, al = split_const(first)
    ih, il = split_const(last)
    bh, bl = split_const(second)
    ch, cl = split_const(third)
    tables = [jnp.asarray(t) for t in (ah, al, ih, il, bh, bl, ch, cl, turn)]

    def vmem(*shape, dtype=F32):
        return pltpu.VMEM(shape, dtype)

    def sems(size):
        return pltpu.SemaphoreType.DMA((2, size))

    operands = (
        tod,
        mode_weight,
        sample_weight,
        pix_row,
        pix_col,
        angle_bin,
        noise_filter.reshape(64, 128),
        mode_coupling,
        *tables,
    )
    tot = pl.pallas_call(
        fused_kernel,
        out_shape=pltpu.VMEM((8, 8, 128), F32),
        in_specs=[sm, sm] + [pl.BlockSpec(memory_space=pl.ANY)] * 17,
        out_specs=vm,
        scratch_shapes=[vmem(*o.shape, dtype=o.dtype) for o in operands]
        + [
            pltpu.SemaphoreType.DMA((17,)),
            vmem(32, 8, 128),
            vmem(ND, 2, 8, 128),
            vmem(32, 8, 128),
            vmem(NT, 4, 8, 128),
            vmem(2, 8, 128),
            vmem(NT, 2, 8, 128),
            vmem(2, 8, 128),
            vmem(ND, 2, 8, 128),
            vmem(NT, 2, 8, 128),
            vmem(NT, 4, 8, 128),
            vmem(NT, 4, 8, 128),
            vmem(32, 8, 128),
            vmem(32, 8, 128),
            vmem(32, 8, 128),
            vmem(32, 8, 128),
            vmem(32, 8, 128),
            vmem(32, 8, 128),
            vmem(32, 8, 128, dtype=jnp.int32),
            vmem(32, 8, 128, dtype=jnp.int32),
            vmem(ND, 3, 16, 128),
            vmem(ND, 3, 16, 128),
            vmem(ND, 16, 128),
            vmem(ND, 16, 128),
            vmem(ND, 3, 16, 128),
            vmem(ND, 16, 128, 128, dtype=BF16),
            vmem(160, 128),
            vmem(96, 128),
            vmem(NT, 5, 8, 128),
            vmem(NT, 3, 8, 128),
            vmem(NT, 5, 8, 128),
            vmem(NT, 3, 8, 128),
            sems(ND),
            sems(NT),
            sems(NT),
            sems(ND),
            sems(NT),
            sems(ND),
            sems(ND),
            sems(NT),
            sems(NT),
        ],
        compiler_params=pltpu.CompilerParams(
            collective_id=0, has_side_effects=True, vmem_limit_bytes=56 << 20
        ),
    )(tile_slot, slot_submap.T, *operands)
    return pl.pallas_call(
        finish_kernel,
        out_shape=(
            jax.ShapeDtypeStruct((1, 3, 8, 128), F32),
            jax.ShapeDtypeStruct((1, 3, 3, 8, 128), F32),
        ),
        in_specs=[vm],
        out_specs=(vm, vm),
    )(pltpu.with_memory_space_constraint(tot, pltpu.VMEM))


def solution(mesh):
    return jax.shard_map(
        body,
        mesh=mesh,
        in_specs=(
            P("det", "tm"),
            P(),
            P(None, "det"),
            P("det", None),
            P("det", "tm"),
            P("det", "tm"),
            P("det", "tm"),
            P("det", "tm"),
            P("tm"),
            P(),
        ),
        out_specs=(P("tm", None, "det", None), P("tm", None, None, "det", None)),
        check_vma=False,
    )
```
